256 devices in a mesh: row: 32 (over z, y), col: 8 (over x, core).
Axes of the slice: x: 4, y: 4, z: 8, core: 2. Of those that a mesh axis runs over, the one named last changes fastest.
Arguments:
- obstacles: float32 [3, 16384], P(None, 'row'), may hold values from 0 to 16
- particles: float32 [3, 8192], P(None, 'row'), may hold values from 0 to 16
- forces: float32 [3, 32, 8192], P(None, None, 'row'), may hold values from -0.8 to 0.8
- neighbours: int32 [64, 32], P('row', 'col'), may hold values from 0 to 127, as said below
- carried: float32 [128, 3, 32, 128], P('row'), may hold values from -6 to 6
- factor: float32 [2, 4096, 128, 3, 128], P(None, 'col', 'row'), may hold values from -0.09375 to 0.09375
- inverses: float32 [2, 4096, 4096], P(None, 'row', 'col'), may hold values from -0.09375 to 0.09375
Outputs:
- solved: float32 [2, 32, 4096], P(None, None, 'col')
- remaining: float32 [128, 3, 32, 128], P('row', None, 'col')
The draws below stay inside these ranges and needn't reach their ends.
Inputs may be any that keep to these rules, and one draw needn't show every extreme that they name: `neighbours`: each particle block lists 32 different obstacle blocks, and every obstacle block is listed by exactly 16 particle blocks.
All inputs are finite; a program needn't handle non-finite values.
Results may differ from the reference program's by a relative error of at most 0.0001.
Values sent between devices are 32-bit elements; how exact they have to be, the bound alone decides.
No kernel may reach another device: no remote copies, remote signals or barrier semaphores. Data moves between devices by JAX's collectives and lax.ppermute only.
A program may use at most 64 MiB of HBM per device.

```python
import jax
import jax.numpy as jnp
from jax import lax

PANEL = 4096
RHS = 32
BLOCK_PTS = 128
GROUP = 128
BLOCKS = 128
POINTS = 16384
PTS_DEV = 512
DIAG_DEV = 128
PARTICLES = 8192
GROUPS = 64
NEIGHBOURS = 32


def draw_neighbours(key, part):
    cycle_count = GROUPS * NEIGHBOURS // BLOCKS
    cycle_keys = jax.random.split(jax.random.fold_in(key, 7), cycle_count)
    orders = jax.vmap(lambda one_key: jax.random.permutation(one_key, BLOCKS))(cycle_keys).astype(jnp.int32)
    listed = orders.reshape(GROUPS, NEIGHBOURS)
    shuffle_keys = jax.random.split(jax.random.fold_in(key, 11), GROUPS)
    within = jax.vmap(lambda one_key: jax.random.permutation(one_key, NEIGHBOURS))(shuffle_keys).astype(jnp.int32)
    return jnp.take_along_axis(listed, within, axis=1).astype(jnp.int32)


def steps_of(stream_key, shape, shards, least, largest):
    loudness = 1.0
    for axis_at, parts in shards:
        steps = jax.random.uniform(jax.random.fold_in(jax.random.fold_in(stream_key, 6), axis_at), (parts,), jnp.float32, least / len(shards), largest / len(shards))
        loudness = loudness * jnp.repeat(jnp.exp(steps), shape[axis_at] // parts).reshape((-1,) + (1,) * (len(shape) - 1 - axis_at))
    return loudness


def gaussian(own_key, shape, width, limit, shards=(), held_as=jnp.bfloat16):
    drawn = jax.random.normal(own_key, shape, jnp.float32) * width
    if len(shards) > 0:
        drawn = steps_of(own_key, shape, shards, -0.22, 0.18) * drawn
    return jnp.clip(drawn, min=-limit, max=limit).astype(held_as)


def setup_inputs(seed: int = 0) -> dict:
    key_of = jax.random.split(jax.random.key(seed), 8)
    return {
        "obstacles": jnp.clip(16.0 * jax.random.uniform(key_of[0], (3, POINTS), jnp.float32) ** steps_of(key_of[0], (3, POINTS), ((1, 32),), -0.2, 0.2), 0.0, 16.0),
        "particles": jnp.clip(16.0 * jax.random.uniform(key_of[1], (3, PARTICLES), jnp.float32) ** steps_of(key_of[1], (3, PARTICLES), ((1, 32),), -0.2, 0.2), 0.0, 16.0),
        "forces": gaussian(key_of[2], (3, RHS, PARTICLES), 0.1, 0.8, ((2, 32),), jnp.float32),
        "neighbours": draw_neighbours(jax.random.fold_in(key_of[7], 71), 0),
        "carried": gaussian(key_of[4], (BLOCKS, 3, RHS, BLOCK_PTS), 1.0, 6.0, ((0, 32),), jnp.float32),
        "factor": gaussian(key_of[5], (2, PANEL, BLOCKS, 3, BLOCK_PTS), PANEL ** -0.5, 0.09375, ((1, 8), (2, 32)), jnp.float32),
        "inverses": gaussian(key_of[6], (2, PANEL, PANEL), PANEL ** -0.5, 0.09375, ((1, 32), (2, 8)), jnp.float32),
    }


soften_square = 1.0
highest = lax.Precision.HIGHEST

def stokeslet(targets, sources, pushes, weight):
    difference = targets[:, :, None] - sources[:, None, :]
    radius = lax.optimization_barrier(jnp.sum(difference * difference, axis=0)) + soften_square
    inverse_cube = lax.rsqrt(radius) / radius * weight
    isotropic = (radius + soften_square) * inverse_cube
    speeds = []
    for left_comp in range(3):
        summed = jnp.einsum('sq,xq->sx', pushes[left_comp], isotropic, precision=highest)
        for right_comp in range(3):
            coupling = difference[left_comp] * difference[right_comp] * inverse_cube
            summed = summed + jnp.einsum('sq,xq->sx', pushes[right_comp], coupling, precision=highest)
        speeds.append(summed)
    return jnp.stack(speeds)

def keep_mask(panel_step, block_count, diag_count, span):
    component = jnp.arange(3, dtype=jnp.int32)[None, :, None, None]
    position = (jnp.arange(block_count, dtype=jnp.int32)[:, None] * BLOCK_PTS + jnp.arange(BLOCK_PTS, dtype=jnp.int32)[None, :]) % span
    position = position[:, None, None, :]
    hidden_rows = (component <= panel_step) & (position < diag_count)
    return jnp.where(hidden_rows, 0.0, 1.0).astype(jnp.float32)

def diag_view(values, component, diag_count, span):
    picked = values[:, component]
    flat = picked.transpose(1, 0, 2).reshape(picked.shape[1], -1, span)
    return flat[:, :, :diag_count].reshape(picked.shape[1], -1)

def near_field(obstacles, particles, forces, neighbours):
    point_blocks = obstacles.reshape(3, BLOCKS, BLOCK_PTS).transpose(1, 0, 2)
    part_blocks = particles.reshape(3, GROUPS, GROUP).transpose(1, 0, 2)
    force_blocks = forces.reshape(3, RHS, GROUPS, GROUP).transpose(2, 0, 1, 3)

    def one_group(running, group_items):
        sources, pushes, listed = group_items

        def one_pair(inner, block_id):
            targets = lax.dynamic_index_in_dim(point_blocks, block_id, 0, keepdims=False)
            speed = stokeslet(targets, sources, pushes, jnp.float32(1.0))
            return (inner.at[block_id].add(speed), None)
        running, _ = lax.scan(one_pair, running, listed)
        return (running, None)
    start_field = jnp.zeros((BLOCKS, 3, RHS, BLOCK_PTS), jnp.float32)
    summed, _ = lax.scan(one_group, start_field, (part_blocks, force_blocks, neighbours))
    return summed

def reference(obstacles, particles, forces, neighbours, carried, factor, inverses):
    rhs_field = carried + near_field(obstacles, particles, forces, neighbours)
    answers = []
    for panel_step in range(2):
        diag_rows = diag_view(rhs_field, panel_step, DIAG_DEV, PTS_DEV)
        answer = jnp.dot(diag_rows, inverses[panel_step], precision=highest, preferred_element_type=jnp.float32)
        answers.append(answer)
        change = jnp.einsum('sj,jbai->basi', answer, factor[panel_step], precision=highest)
        rhs_field = rhs_field - change * keep_mask(panel_step, BLOCKS, DIAG_DEV, PTS_DEV)
    return (jnp.stack(answers), rhs_field)
```

```python
import jax
import jax.numpy as jnp
from jax import lax
from jax.sharding import PartitionSpec as P

ROWS = 32
COLS = 8
BLOCKS_DEV = 4
BLOCK_PTS = 128
SLICE = 32
RHS = 32
COMPS = 3

highest = lax.Precision.HIGHEST


def col_sum(part):
    pair = part + lax.ppermute(part, "col", [(i, i ^ 1) for i in range(COLS)])
    others = [
        lax.ppermute(pair, "col", [(i, (i + step) % COLS) for i in range(COLS)])
        for step in (2, 6, 4)
    ]
    return pair + others[0] + (others[1] + others[2])


def exchange_inputs(particles, forces, neighbours):
    col = lax.axis_index("col")
    rhs_share = RHS // COLS
    mine = lax.dynamic_slice_in_dim(forces, col * rhs_share, rhs_share, 1)
    mine = mine.reshape(COMPS, rhs_share, COLS, SLICE).transpose(2, 1, 0, 3)
    mine = mine.reshape(COLS, rhs_share, COMPS * SLICE)
    places = particles.reshape(COMPS, COLS, SLICE).transpose(1, 0, 2)
    listed = jnp.repeat(neighbours, COLS // 2, axis=0).astype(jnp.float32)
    listed = jnp.pad(listed, ((0, 0), (0, SLICE - listed.shape[1])))[:, None, :]
    payload = jnp.concatenate([mine, jnp.concatenate([places, listed], axis=1)], axis=2)
    sent = jnp.broadcast_to(payload[None], (ROWS, COLS, rhs_share, 128))
    sent = sent.reshape(ROWS * COLS, rhs_share, 128)
    return lax.all_to_all(sent, ("row", "col"), 0, 0, tiled=True)


def near_part(obstacles, got):
    row = lax.axis_index("row")
    pushes = got.reshape(ROWS, RHS, 128)[:, :, : COMPS * SLICE]
    pushes = pushes.reshape(ROWS, RHS, COMPS, SLICE).transpose(2, 1, 0, 3)
    pushes = pushes.reshape(COMPS, RHS, ROWS * SLICE)
    tails = got.reshape(ROWS, COLS, 4, 128)
    sources = tails[:, 0, :COMPS, COMPS * SLICE :].transpose(1, 0, 2).reshape(COMPS, ROWS * SLICE)
    lists = tails[:, :, COMPS, COMPS * SLICE : COMPS * SLICE + 4].reshape(ROWS, -1)
    own = (row * BLOCKS_DEV + jnp.arange(BLOCKS_DEV, dtype=jnp.int32)).astype(jnp.float32)
    held = jnp.any(lists[:, :, None] == own[None, None, :], axis=1).astype(jnp.float32)
    weight = jnp.repeat(held, SLICE, axis=0)
    weight = jnp.repeat(weight, BLOCK_PTS, axis=1)
    difference = obstacles[:, None, :] - sources[:, :, None]
    radius = jnp.sum(difference * difference, axis=0) + 1.0
    cube = lax.rsqrt(radius) / radius * weight
    iso = (radius + 1.0) * cube
    speeds = []
    for left in range(COMPS):
        total = jnp.dot(pushes[left], iso, precision=highest)
        for right in range(COMPS):
            coupling = difference[left] * difference[right] * cube
            total = total + jnp.dot(pushes[right], coupling, precision=highest)
        speeds.append(total)
    out = jnp.stack(speeds)
    return out.reshape(COMPS, RHS, BLOCKS_DEV, BLOCK_PTS).transpose(2, 0, 1, 3)


def solve(diag, inverse):
    part = jnp.dot(diag, inverse, precision=highest).reshape(ROWS, 4, 128)
    got = lax.all_to_all(part, "row", 0, 0, tiled=True)
    mine = jnp.broadcast_to(jnp.sum(got, axis=0)[None], (ROWS, 4, 128))
    return lax.all_to_all(mine, "row", 0, 0, tiled=True).reshape(RHS, 512)


def body(obstacles, particles, forces, neighbours, carried, factor, inverses):
    col = lax.axis_index("col")
    rhs_share = RHS // COLS
    got = exchange_inputs(particles, forces, neighbours)
    near = near_part(obstacles, got)
    diag0 = carried[0, 0] + col_sum(near[0, 0])
    first = solve(diag0, inverses[0])
    diag1_part = near[0, 1] - jnp.dot(first, factor[0, :, 0, 1, :], precision=highest)
    diag1 = carried[0, 1] + col_sum(diag1_part)
    change0 = jnp.einsum("sj,jbai->basi", first, factor[0], precision=highest)
    second = solve(diag1, inverses[1])
    change1 = jnp.einsum("sj,jbai->basi", second, factor[1], precision=highest)
    part = near - (change0 + change1)
    part = part.at[0, 0].set(near[0, 0]).at[0, 1].set(diag1_part)
    part = part.reshape(BLOCKS_DEV, COMPS, COLS, rhs_share, BLOCK_PTS).transpose(2, 0, 1, 3, 4)
    back = lax.all_to_all(part, "col", 0, 0, tiled=True)
    share = lax.dynamic_slice_in_dim(carried, col * rhs_share, rhs_share, 2)
    remaining = share + jnp.sum(back, axis=0)
    return (jnp.stack([first, second]), remaining)


def solution(mesh):
    in_specs = (
        P(None, "row"),
        P(None, "row"),
        P(None, None, "row"),
        P("row", "col"),
        P("row", None, None, None),
        P(None, "col", "row", None, None),
        P(None, "row", "col"),
    )
    out_specs = (P(None, None, "col"), P("row", None, "col", None))
    return jax.shard_map(body, mesh=mesh, in_specs=in_specs, out_specs=out_specs, check_vma=False)
```

```python
import functools

import jax
import jax.numpy as jnp
from jax import lax
from jax.experimental import pallas as pl
from jax.experimental.pallas import tpu as pltpu
from jax.sharding import PartitionSpec as P

ROWS = 32
COLS = 8
BLOCKS_DEV = 4
BLOCK_PTS = 128
SLICE = 32
RHS = 32
COMPS = 3

highest = lax.Precision.HIGHEST


def col_sum(part):
    pair = part + lax.ppermute(part, "col", [(i, i ^ 1) for i in range(COLS)])
    others = [
        lax.ppermute(pair, "col", [(i, (i + step) % COLS) for i in range(COLS)])
        for step in (2, 6, 4)
    ]
    return pair + others[0] + (others[1] + others[2])


def exchange_inputs(particles, forces, neighbours):
    col = lax.axis_index("col")
    rhs_share = RHS // COLS
    mine = lax.dynamic_slice_in_dim(forces, col * rhs_share, rhs_share, 1)
    mine = mine.reshape(COMPS, rhs_share, COLS, SLICE).transpose(2, 1, 0, 3)
    mine = mine.reshape(COLS, rhs_share, COMPS * SLICE)
    places = particles.reshape(COMPS, COLS, SLICE).transpose(1, 0, 2)
    listed = jnp.repeat(neighbours, COLS // 2, axis=0).astype(jnp.float32)
    listed = jnp.pad(listed, ((0, 0), (0, SLICE - listed.shape[1])))[:, None, :]
    payload = jnp.concatenate([mine, jnp.concatenate([places, listed], axis=1)], axis=2)
    sent = jnp.broadcast_to(payload[None], (ROWS, COLS, rhs_share, 128))
    sent = sent.reshape(ROWS * COLS, rhs_share, 128)
    return lax.all_to_all(sent, ("row", "col"), 0, 0, tiled=True)


PAIRS = ((0, 0), (1, 1), (2, 2), (0, 1), (0, 2), (1, 2))

def halves(value):
    high = value.astype(jnp.bfloat16)
    return high, (value - high.astype(jnp.float32)).astype(jnp.bfloat16)

def near_kernel(held_ref, got_ref, points_ref, out_ref, push, source, high, low):
    lane = lax.broadcasted_iota(jnp.int32, (RHS, 128), 1) // SLICE
    for quad in range(8):
        for comp in range(COMPS):
            joined = None
            for at in range(4):
                piece = got_ref[4 * quad + at]
                turn = (SLICE * (at - comp)) % 128
                piece = pltpu.roll(piece, turn, axis=1) if turn else piece
                joined = piece if joined is None else jnp.where(lane == at, piece, joined)
            top, rest = halves(joined)
            cols = pl.ds(128 * (quad % 2), 128)
            push[comp, quad // 2, 0:32, cols] = top
            push[comp, quad // 2, 32:64, cols] = rest
    heads = got_ref[:, 0:8, :].reshape(ROWS * 8, 128).T
    for group in range(ROWS):
        for comp in range(COMPS):
            column = heads[96:128, 8 * group + comp : 8 * group + comp + 1]
            source[comp, pl.ds(SLICE * group, SLICE), :] = jnp.broadcast_to(column, (SLICE, 128))
    for half in range(2):
        totals = [None] * COMPS
        for tile in range(4):
            slot = tile % 2
            for block in range(2):
                cols = pl.ds(128 * block, 128)
                points = [points_ref[c : c + 1, pl.ds(256 * half + 128 * block, 128)] for c in range(COMPS)]
                for at in range(8):
                    group = 8 * tile + at
                    rows = pl.ds(SLICE * at, SLICE)
                    diff = [points[c] - source[c, pl.ds(SLICE * group, SLICE), :] for c in range(COMPS)]
                    radius = diff[0] * diff[0] + diff[1] * diff[1] + diff[2] * diff[2] + 1.0
                    root = lax.rsqrt(radius)
                    cube = root * root * root * held_ref[4 * group + 2 * half + block]
                    iso = (radius + 1.0) * cube
                    scaled = [diff[0] * cube, diff[1] * cube]
                    for n, (a, b) in enumerate(PAIRS):
                        if a == b:
                            value = diff[a] * (scaled[a] if a < 2 else diff[a] * cube) + iso
                        else:
                            value = scaled[a] * diff[b]
                        top, rest = halves(value)
                        high[slot, n, rows, cols] = top
                        low[slot, n, rows, cols] = rest
            for n, (a, b) in enumerate(PAIRS):
                left = push[b, tile] if a == b else jnp.concatenate([push[b, tile], push[a, tile]], axis=0)
                full = jnp.dot(left, high[slot, n], preferred_element_type=jnp.float32)
                left = push[b, tile, 0:32] if a == b else jnp.concatenate([push[b, tile, 0:32], push[a, tile, 0:32]], axis=0)
                rest = jnp.dot(left, low[slot, n], preferred_element_type=jnp.float32)
                add = full[0:32] + full[32:64] + rest[0:32]
                totals[a] = add if totals[a] is None else totals[a] + add
                if a != b:
                    add = full[64:96] + full[96:128] + rest[32:64]
                    totals[b] = add if totals[b] is None else totals[b] + add
        for comp in range(COMPS):
            out_ref[2 * half, comp] = totals[comp][:, 0:128]
            out_ref[2 * half + 1, comp] = totals[comp][:, 128:256]

def near_call(held, got, obstacles):
    return pl.pallas_call(
        near_kernel,
        out_shape=jax.ShapeDtypeStruct((4, COMPS, RHS, 128), jnp.float32),
        in_specs=[pl.BlockSpec(memory_space=pltpu.SMEM), pl.BlockSpec(memory_space=pltpu.VMEM), pl.BlockSpec(memory_space=pltpu.VMEM)],
        out_specs=pl.BlockSpec(memory_space=pltpu.VMEM),
        scratch_shapes=[
            pltpu.VMEM((COMPS, 4, 64, 256), jnp.bfloat16),
            pltpu.VMEM((COMPS, ROWS * SLICE, 128), jnp.float32),
            pltpu.VMEM((2, 6, 256, 256), jnp.bfloat16),
            pltpu.VMEM((2, 6, 256, 256), jnp.bfloat16),
        ],
        name="near_field",
    )(held, got, obstacles)


def near_part(obstacles, got):
    row = lax.axis_index("row")
    lists = got.reshape(ROWS, COLS, 4, 128)[:, :, COMPS, COMPS * SLICE : COMPS * SLICE + 4]
    lists = lists.reshape(ROWS, -1)
    own = (row * BLOCKS_DEV + jnp.arange(BLOCKS_DEV, dtype=jnp.int32)).astype(jnp.float32)
    held = jnp.any(lists[:, :, None] == own[None, None, :], axis=1).astype(jnp.float32)
    return near_call(held.reshape(-1), got.reshape(ROWS, RHS, 128), obstacles)


def change_kernel(panel, split, answer_ref, factor_ref, base_ref, out_ref):
    answer = jnp.concatenate([answer_ref[:, q, :] for q in range(4)], axis=1)
    top, rest = halves(answer)
    both = jnp.concatenate([top, rest], axis=0)
    for comp in range(COMPS):
        for block in range(BLOCKS_DEV):
            value = base_ref[block, comp]
            if block > 0 or comp > panel:
                cols = factor_ref[pl.ds(BLOCKS_DEV * comp + block, 512, stride=12), :]
                high, low = halves(cols)
                full = jnp.dot(both, high, preferred_element_type=jnp.float32)
                part = jnp.dot(top, low, preferred_element_type=jnp.float32)
                value = value - (full[0:32] + full[32:64] + part)
            if split:
                for part_at in range(COLS):
                    out_ref[part_at, block, comp] = value[4 * part_at : 4 * part_at + 4]
            else:
                out_ref[block, comp] = value


def change_call(panel, split, answer, factor_rows, base):
    shape = (COLS, BLOCKS_DEV, COMPS, 4, 128) if split else (BLOCKS_DEV, COMPS, RHS, 128)
    return pl.pallas_call(
        functools.partial(change_kernel, panel, split),
        grid=(1,),
        out_shape=jax.ShapeDtypeStruct(shape, jnp.float32),
        in_specs=[
            pl.BlockSpec((RHS, 4, 128), lambda i: (0, 0, 0)),
            pl.BlockSpec((None, 6144, 128), lambda i: (panel, 0, 0)),
            pl.BlockSpec((BLOCKS_DEV, COMPS, RHS, 128), lambda i: (0, 0, 0, 0)),
        ],
        out_specs=pl.BlockSpec(shape, lambda i: (0,) * len(shape)),
        name="change",
    )(answer, factor_rows, base)


def solve(diag, inverse):
    part = jnp.dot(diag, inverse, precision=highest).reshape(ROWS, 4, 128)
    got = lax.all_to_all(part, "row", 0, 0, tiled=True)
    mine = jnp.broadcast_to(jnp.sum(got, axis=0)[None], (ROWS, 4, 128))
    return lax.all_to_all(mine, "row", 0, 0, tiled=True)


def body(obstacles, particles, forces, neighbours, carried, factor, inverses):
    col = lax.axis_index("col")
    rhs_share = RHS // COLS
    got = exchange_inputs(particles, forces, neighbours)
    near = near_part(obstacles, got)
    diag0 = carried[0, 0] + col_sum(near[0, 0])
    first = solve(diag0, inverses[0])
    rows = factor.transpose(0, 1, 3, 2, 4).reshape(2, 6144, 128)
    answer = first.reshape(RHS, 512)
    diag1_part = near[0, 1] - jnp.dot(answer, factor[0, :, 0, 1, :], precision=highest)
    diag1 = carried[0, 1] + col_sum(diag1_part)
    part = change_call(0, False, first, rows, near)
    second = solve(diag1, inverses[1])
    part = change_call(1, True, second, rows, part)
    back = lax.all_to_all(part, "col", 0, 0, tiled=True)
    share = lax.dynamic_slice_in_dim(carried, col * rhs_share, rhs_share, 2)
    remaining = share + jnp.sum(back, axis=0)
    return (jnp.stack([first, second]).reshape(2, RHS, 512), remaining)


def solution(mesh):
    in_specs = (
        P(None, "row"),
        P(None, "row"),
        P(None, None, "row"),
        P("row", "col"),
        P("row", None, None, None),
        P(None, "col", "row", None, None),
        P(None, "row", "col"),
    )
    out_specs = (P(None, None, "col"), P("row", None, "col", None))
    return jax.shard_map(body, mesh=mesh, in_specs=in_specs, out_specs=out_specs, check_vma=False)
```

```python
import functools

import jax
import jax.numpy as jnp
from jax import lax
from jax.experimental import pallas as pl
from jax.experimental.pallas import tpu as pltpu
from jax.sharding import PartitionSpec as P

ROWS = 32
COLS = 8
BLOCKS_DEV = 4
SLICE = 32
RHS = 32
COMPS = 3
PAIRS = ((0, 0), (1, 1), (2, 2), (0, 1), (0, 2), (1, 2))
SHARE = RHS // COLS
COLUMNS = 512

ON_CHIP = pl.BlockSpec(memory_space=pltpu.VMEM)
IN_PLACE = pl.BlockSpec(memory_space=pltpu.HBM)
GRANT = pltpu.CompilerParams(vmem_limit_bytes=16 << 20)


def kept(shape, dtype=jnp.float32):
    return pltpu.VMEM(shape, dtype)


def keep(array):
    return pltpu.with_memory_space_constraint(array, pltpu.VMEM)


def stay(array):
    return pltpu.with_memory_space_constraint(array, pltpu.HBM)


def halves(value):
    high = value.astype(jnp.bfloat16)
    return high, (value - high.astype(jnp.float32)).astype(jnp.bfloat16)


def product(left, high, low):
    top, rest = halves(left)
    both = jnp.concatenate([top, rest], axis=0)
    full = jnp.dot(both, high, preferred_element_type=jnp.float32)
    part = jnp.dot(top, low, preferred_element_type=jnp.float32)
    count = left.shape[0]
    return full[:count] + full[count:] + part


def payload_kernel(
    forces_hbm, particles_hbm, neighbours_hbm, out_hbm, forces_ref, particles_ref, neighbours_ref, sent, read, wrote
):
    col = lax.axis_index("col")
    start = pl.multiple_of((col // 2) * 8, 8)
    copies = [
        pltpu.make_async_copy(forces_hbm.at[:, pl.ds(start, 8), :], forces_ref, read.at[0]),
        pltpu.make_async_copy(particles_hbm, particles_ref, read.at[1]),
        pltpu.make_async_copy(neighbours_hbm, neighbours_ref, read.at[2]),
    ]
    for copy in copies:
        copy.start()
    lane = lax.broadcasted_iota(jnp.int32, (8, 128), 1)
    line = lax.broadcasted_iota(jnp.int32, (8, 128), 0)
    odd = jnp.full((8, 128), col % 2, jnp.int32) == 1
    for copy in copies:
        copy.wait()
    for half in range(2):
        sides = []
        for comp in range(COMPS):
            eight = forces_ref[comp, :, pl.ds(128 * half, 128)]
            sides.append(jnp.where(odd, pltpu.roll(eight, 4, axis=0), eight))
        place = jnp.concatenate(
            [particles_ref[:, pl.ds(128 * half, 128)], jnp.zeros((5, 128), jnp.float32)], axis=0
        )
        listed = jnp.full((8, 128), -1.0, jnp.float32)
        for entry in range(4):
            name = jnp.full((8, 128), neighbours_ref[half, entry], jnp.int32).astype(jnp.float32)
            listed = jnp.where(lane == 96 + entry, name, listed)
        for quarter in range(4):
            value = None
            for at, piece in enumerate([*sides, place]):
                turn = (SLICE * (at - quarter)) % 128
                piece = pltpu.roll(piece, turn, axis=1) if turn else piece
                value = piece if value is None else jnp.where(lane >= SLICE * at, piece, value)
            value = jnp.where((lane >= 96) & (line == 3), listed, value)
            sent[4 * half + quarter] = value[0:4]
    copies = [pltpu.make_async_copy(sent, out_hbm.at[row], wrote.at[row]) for row in range(ROWS)]
    for copy in copies:
        copy.start()
    for copy in copies:
        copy.wait()


def payload(forces, particles, neighbours):
    return pl.pallas_call(
        payload_kernel,
        out_shape=pltpu.HBM((ROWS, COLS, SHARE, 128), jnp.float32),
        in_specs=[IN_PLACE] * 3,
        out_specs=IN_PLACE,
        scratch_shapes=[
            pltpu.VMEM((COMPS, 8, 256), jnp.float32),
            pltpu.VMEM((COMPS, 256), jnp.float32),
            pltpu.SMEM((2, 4), jnp.int32),
            pltpu.VMEM((COLS, SHARE, 128), jnp.float32),
            pltpu.SemaphoreType.DMA((3,)),
            pltpu.SemaphoreType.DMA((ROWS,)),
        ],
        name="payload",
        compiler_params=GRANT,
    )(stay(forces), stay(particles), stay(neighbours))


def prepare_kernel(
    factor_ref, inverses_ref, carried_ref, fh_ref, fl_ref, dh_ref, dl_ref, ih_ref, il_ref, mine_ref
):
    for panel in range(2):
        for comp in range(COMPS):
            for block in range(BLOCKS_DEV):
                rows = pl.ds(BLOCKS_DEV * comp + block, COLUMNS, stride=COMPS * BLOCKS_DEV)
                high, low = halves(factor_ref[panel, rows, :])
                pair = 2 * comp + block // 2
                lanes = pl.ds(128 * (block % 2), 128)
                fh_ref[panel, pair, :, lanes] = high
                fl_ref[panel, pair, :, lanes] = low
                if panel == 0 and comp == 1 and block == 0:
                    dh_ref[...] = high
                    dl_ref[...] = low
        high, low = halves(inverses_ref[panel])
        ih_ref[panel] = high
        il_ref[panel] = low
    owner = lax.broadcasted_iota(jnp.int32, (RHS, 128), 0) // SHARE
    own = owner == jnp.full((RHS, 128), lax.axis_index("col"), jnp.int32)
    for block in range(BLOCKS_DEV):
        for comp in range(COMPS):
            mine_ref[block, comp] = jnp.where(own, carried_ref[block, comp], 0.0)


def prepare(factor_rows, inverses, carried):
    panels = (2, 2 * COMPS, COLUMNS, 256)
    return pl.pallas_call(
        prepare_kernel,
        out_shape=(
            pltpu.HBM(panels, jnp.bfloat16),
            pltpu.HBM(panels, jnp.bfloat16),
            kept((COLUMNS, 128), jnp.bfloat16),
            kept((COLUMNS, 128), jnp.bfloat16),
            kept(inverses.shape, jnp.bfloat16),
            kept(inverses.shape, jnp.bfloat16),
            kept(carried.shape),
        ),
        in_specs=[ON_CHIP] * 3,
        out_specs=(ON_CHIP,) * 7,
        name="prepare",
        compiler_params=GRANT,
    )(factor_rows, inverses, carried)


def couple(blocks, points_ref, flags_ref, push_ref, source_ref, high, low):
    width = 128 * len(blocks)
    totals = [None] * COMPS
    for tile in range(4):
        slot = tile % 2
        for where, block in enumerate(blocks):
            lanes = pl.ds(128 * where, 128)
            points = [points_ref[c : c + 1, pl.ds(128 * block, 128)] for c in range(COMPS)]
            flags = flags_ref[block : block + 1, :]
            for at in range(8):
                group = 8 * tile + at
                rows = pl.ds(SLICE * at, SLICE)
                spots = pl.ds(SLICE * group, SLICE)
                diff = [points[c] - source_ref[c, spots, :] for c in range(COMPS)]
                flag = jnp.broadcast_to(flags[:, 8 * group : 8 * group + 1], (SLICE, 128))
                radius = diff[0] * diff[0] + diff[1] * diff[1] + diff[2] * diff[2] + 1.0
                root = lax.rsqrt(radius)
                cube = root * root * root * flag
                iso = (radius + 1.0) * cube
                scaled = [diff[0] * cube, diff[1] * cube, diff[2] * cube]
                for n, (a, b) in enumerate(PAIRS):
                    value = scaled[a] * diff[b]
                    top, rest = halves(value + iso if a == b else value)
                    high[slot, n, rows, lanes] = top
                    low[slot, n, rows, lanes] = rest
        for n, (a, b) in enumerate(PAIRS):
            if a == b:
                left, first = push_ref[b, tile], push_ref[b, tile, 0:32]
            else:
                left = jnp.concatenate([push_ref[b, tile], push_ref[a, tile]], axis=0)
                first = jnp.concatenate(
                    [push_ref[b, tile, 0:32], push_ref[a, tile, 0:32]], axis=0
                )
            full = jnp.dot(left, high[slot, n, :, 0:width], preferred_element_type=jnp.float32)
            rest = jnp.dot(first, low[slot, n, :, 0:width], preferred_element_type=jnp.float32)
            add = full[0:32] + full[32:64] + rest[0:32]
            totals[a] = add if totals[a] is None else totals[a] + add
            if a != b:
                add = full[64:96] + full[96:128] + rest[32:64]
                totals[b] = add if totals[b] is None else totals[b] + add
    return totals


def near_first_kernel(
    got_ref, points_ref, mine_ref, out_ref, spread_ref, push_ref, source_ref, flags_ref, high, low
):
    lane = lax.broadcasted_iota(jnp.int32, (RHS, 128), 1) // SLICE
    for quad in range(8):
        for comp in range(COMPS):
            joined = None
            for at in range(4):
                piece = got_ref[pl.ds(RHS * (4 * quad + at), RHS), :]
                turn = (SLICE * (at - comp)) % 128
                piece = pltpu.roll(piece, turn, axis=1) if turn else piece
                joined = piece if joined is None else jnp.where(lane == at, piece, joined)
            top, rest = halves(joined)
            lanes = pl.ds(128 * (quad % 2), 128)
            push_ref[comp, quad // 2, 0:32, lanes] = top
            push_ref[comp, quad // 2, 32:64, lanes] = rest
    for comp in range(COMPS):
        places = got_ref[pl.ds(comp, ROWS, stride=RHS), :].T
        for group in range(ROWS):
            column = places[96:128, group : group + 1]
            source_ref[comp, pl.ds(SLICE * group, SLICE), :] = jnp.broadcast_to(column, (SLICE, 128))
    lists = got_ref[pl.ds(3, ROWS * COLS, stride=4), :].T[96:104, :]
    first = BLOCKS_DEV * lax.axis_index("row")
    for block in range(BLOCKS_DEV):
        name = jnp.full(lists.shape, first + block, jnp.int32).astype(jnp.float32)
        found = jnp.where(lists == name, 1.0, 0.0)
        for step in (1, 2, 4):
            found = jnp.maximum(found, pltpu.roll(found, ROWS * COLS - step, axis=1))
        flags_ref[block : block + 1, :] = jnp.max(found, axis=0, keepdims=True)
    totals = couple((0,), points_ref, flags_ref, push_ref, source_ref, high, low)
    for comp in range(COMPS):
        value = totals[comp] + mine_ref[0, comp]
        out_ref[comp] = value
        if comp == 0:
            for part in range(COLS):
                spread_ref[part] = value


def near_first(got, points, mine):
    return pl.pallas_call(
        near_first_kernel,
        out_shape=(
            kept((COMPS, RHS, 128)),
            kept((COLS, RHS, 128)),
            kept((COMPS, 4, 64, 256), jnp.bfloat16),
            kept((COMPS, ROWS * SLICE, 128)),
            kept((BLOCKS_DEV, 256)),
        ),
        in_specs=[ON_CHIP] * 3,
        out_specs=(ON_CHIP,) * 5,
        scratch_shapes=[pltpu.VMEM((2, 6, 256, 128), jnp.bfloat16)] * 2,
        name="near_first",
        compiler_params=GRANT,
    )(keep(got), points, keep(mine))


def near_rest_kernel(
    points_ref, mine_ref, push_ref, source_ref, flags_ref, out_ref, high, low
):
    for blocks in ((1, 2), (3,)):
        totals = couple(blocks, points_ref, flags_ref, push_ref, source_ref, high, low)
        for where, block in enumerate(blocks):
            for comp in range(COMPS):
                value = totals[comp][:, 128 * where : 128 * where + 128]
                out_ref[block - 1, comp] = value + mine_ref[block, comp]


def near_rest(points, mine, push, source, flags):
    return pl.pallas_call(
        near_rest_kernel,
        out_shape=kept((BLOCKS_DEV - 1, COMPS, RHS, 128)),
        in_specs=[ON_CHIP] * 5,
        out_specs=ON_CHIP,
        scratch_shapes=[pltpu.VMEM((2, 6, 256, 256), jnp.bfloat16)] * 2,
        name="near_rest",
        compiler_params=GRANT,
    )(points, keep(mine), keep(push), keep(source), keep(flags))


def solve_kernel(panel, parts_ref, ih_ref, il_ref, out_ref):
    diag = parts_ref[0]
    for part in range(1, COLS):
        diag = diag + parts_ref[part]
    value = product(diag, ih_ref[panel], il_ref[panel])
    for quarter in range(4):
        out_ref[pl.ds(quarter, RHS, stride=4), :] = value[:, 128 * quarter : 128 * quarter + 128]


def add_kernel(got_ref, out_ref):
    total = got_ref[0:8]
    for at in range(1, 16):
        total = total + got_ref[8 * at : 8 * at + 8]
    total = total + pltpu.roll(total, 4, axis=0)
    for at in range(16):
        out_ref[8 * at : 8 * at + 8] = total


def solve(panel, parts, ih, il):
    partial = pl.pallas_call(
        functools.partial(solve_kernel, panel),
        out_shape=kept((RHS * 4, 128)),
        in_specs=[ON_CHIP] * 3,
        out_specs=ON_CHIP,
        name="solve",
        compiler_params=GRANT,
    )(keep(parts), keep(ih), keep(il))
    got = lax.all_to_all(partial.reshape(ROWS, 4, 128), "row", 0, 0, tiled=True)
    summed = pl.pallas_call(
        add_kernel,
        out_shape=kept((ROWS * 4, 128)),
        in_specs=[ON_CHIP],
        out_specs=ON_CHIP,
        name="add",
        compiler_params=GRANT,
    )(keep(got.reshape(ROWS * 4, 128)))
    got = lax.all_to_all(summed.reshape(ROWS, 4, 128), "row", 0, 0, tiled=True)
    return got.reshape(ROWS * 4, 128)


def whole(answer_ref):
    return jnp.concatenate(
        [answer_ref[pl.ds(quarter, RHS, stride=4), :] for quarter in range(4)], axis=1
    )


def diagonal_kernel(answer_ref, dh_ref, dl_ref, near_ref, out_ref):
    change = product(whole(answer_ref), dh_ref[...], dl_ref[...])
    value = near_ref[1] - change
    for part in range(COLS):
        out_ref[part] = value


def diagonal(answer, dh, dl, near):
    return pl.pallas_call(
        diagonal_kernel,
        out_shape=kept((COLS, RHS, 128)),
        in_specs=[ON_CHIP] * 4,
        out_specs=ON_CHIP,
        name="diagonal",
        compiler_params=GRANT,
    )(keep(answer), keep(dh), keep(dl), keep(near))


def changes(panel, answer_ref, fh_hbm, fl_hbm, high, low, read):
    count = 2 * COMPS
    copies = []
    for at in range(count):
        copies.append(pltpu.make_async_copy(fh_hbm.at[panel, at], high.at[at], read.at[at]))
        copies.append(pltpu.make_async_copy(fl_hbm.at[panel, at], low.at[at], read.at[count + at]))
    for copy in copies:
        copy.start()
    answer = whole(answer_ref)
    for comp in range(COMPS):
        for pair in range(2):
            at = 2 * comp + pair
            copies[2 * at].wait()
            copies[2 * at + 1].wait()
            value = product(answer, high[at], low[at])
            for where in range(2):
                block = 2 * pair + where
                hidden = block == 0 and comp <= panel
                yield block, comp, None if hidden else value[:, 128 * where : 128 * where + 128]


STREAM = [
    pltpu.VMEM((2 * COMPS, COLUMNS, 256), jnp.bfloat16),
    pltpu.VMEM((2 * COMPS, COLUMNS, 256), jnp.bfloat16),
    pltpu.SemaphoreType.DMA((4 * COMPS,)),
]


def change_first_kernel(answer_ref, fh_hbm, fl_hbm, first_ref, rest_ref, out_ref, *stream):
    for block, comp, value in changes(0, answer_ref, fh_hbm, fl_hbm, *stream):
        base = first_ref[comp] if block == 0 else rest_ref[block - 1, comp]
        out_ref[block, comp] = base if value is None else base - value


def change_first(answer, fh, fl, first, rest):
    return pl.pallas_call(
        change_first_kernel,
        out_shape=kept((BLOCKS_DEV, COMPS, RHS, 128)),
        in_specs=[ON_CHIP, IN_PLACE, IN_PLACE, ON_CHIP, ON_CHIP],
        out_specs=ON_CHIP,
        scratch_shapes=STREAM,
        name="change_first",
        compiler_params=GRANT,
    )(keep(answer), stay(fh), stay(fl), keep(first), keep(rest))


def change_second_kernel(answer_ref, fh_hbm, fl_hbm, base_ref, out_ref, *stream):
    for block, comp, value in changes(1, answer_ref, fh_hbm, fl_hbm, *stream):
        base = base_ref[block, comp]
        value = base if value is None else base - value
        for part in range(COLS):
            out_ref[part, block, comp] = value[SHARE * part : SHARE * part + SHARE]


def change_second(answer, fh, fl, base):
    return pl.pallas_call(
        change_second_kernel,
        out_shape=pltpu.HBM((COLS, BLOCKS_DEV, COMPS, SHARE, 128), jnp.float32),
        in_specs=[ON_CHIP, IN_PLACE, IN_PLACE, ON_CHIP],
        out_specs=ON_CHIP,
        scratch_shapes=STREAM,
        name="change_second",
        compiler_params=GRANT,
    )(keep(answer), stay(fh), stay(fl), keep(base))


def body(obstacles, particles, forces, neighbours, carried, factor, inverses):
    sent = payload(forces, particles, neighbours).reshape(ROWS * COLS, SHARE, 128)
    got = lax.all_to_all(sent, ("row", "col"), 0, 0, tiled=True).reshape(ROWS * RHS, 128)
    rows = factor.transpose(0, 1, 3, 2, 4).reshape(2, COLUMNS * COMPS * BLOCKS_DEV, 128)
    fh, fl, dh, dl, ih, il, mine = prepare(rows, inverses, carried)
    near0, spread, push, source, flags = near_first(got, obstacles, mine)
    parts = lax.all_to_all(spread, "col", 0, 0, tiled=True)
    rest = near_rest(obstacles, mine, push, source, flags)
    first = solve(0, parts, ih, il)
    first, rest = lax.optimization_barrier((first, rest))
    parts = lax.all_to_all(diagonal(first, dh, dl, near0), "col", 0, 0, tiled=True)
    part = change_first(first, fh, fl, near0, rest)
    second = solve(1, parts, ih, il)
    part = change_second(second, fh, fl, part)
    back = lax.all_to_all(part, "col", 0, 0, tiled=True)
    answers = jnp.stack([first.reshape(RHS, COLUMNS), second.reshape(RHS, COLUMNS)])
    return (answers, jnp.sum(back, axis=0))


def solution(mesh):
    in_specs = (
        P(None, "row"),
        P(None, "row"),
        P(None, None, "row"),
        P("row", "col"),
        P("row", None, None, None),
        P(None, "col", "row", None, None),
        P(None, "row", "col"),
    )
    out_specs = (P(None, None, "col"), P("row", None, "col", None))
    return jax.shard_map(body, mesh=mesh, in_specs=in_specs, out_specs=out_specs, check_vma=False)
```

```python
import functools

import jax
import jax.numpy as jnp
from jax import lax
from jax.experimental import pallas as pl
from jax.experimental.pallas import tpu as pltpu
from jax.sharding import PartitionSpec as P

ROWS = 32
COLS = 8
BLOCKS_DEV = 4
SLICE = 32
RHS = 32
COMPS = 3
PAIRS = ((0, 0), (1, 1), (2, 2), (0, 1), (0, 2), (1, 2))
SHARE = RHS // COLS
COLUMNS = 512
RING = 4
DEPTH = 8
EIGHT = RHS // RING

ON_CHIP = pl.BlockSpec(memory_space=pltpu.VMEM)
IN_PLACE = pl.BlockSpec(memory_space=pltpu.HBM)
GRANT = pltpu.CompilerParams(vmem_limit_bytes=16 << 20)


def kept(shape, dtype=jnp.float32):
    return pltpu.VMEM(shape, dtype)


def keep(array):
    return pltpu.with_memory_space_constraint(array, pltpu.VMEM)


def stay(array):
    return pltpu.with_memory_space_constraint(array, pltpu.HBM)


def halves(value):
    high = value.astype(jnp.bfloat16)
    return high, (value - high.astype(jnp.float32)).astype(jnp.bfloat16)


def product(left, high, low):
    top, rest = halves(left)
    both = jnp.concatenate([top, rest], axis=0)
    full = jnp.dot(both, high, preferred_element_type=jnp.float32)
    part = jnp.dot(top, low, preferred_element_type=jnp.float32)
    count = left.shape[0]
    return full[:count] + full[count:] + part


def payload_kernel(
    forces_hbm, particles_hbm, neighbours_hbm, out_hbm, forces_ref, particles_ref, neighbours_ref, sent, read, wrote
):
    col = lax.axis_index("col")
    start = pl.multiple_of((col // 2) * 8, 8)
    copies = [
        pltpu.make_async_copy(forces_hbm.at[:, pl.ds(start, 8), :], forces_ref, read.at[0]),
        pltpu.make_async_copy(particles_hbm, particles_ref, read.at[1]),
        pltpu.make_async_copy(neighbours_hbm, neighbours_ref, read.at[2]),
    ]
    for copy in copies:
        copy.start()
    lane = lax.broadcasted_iota(jnp.int32, (8, 128), 1)
    line = lax.broadcasted_iota(jnp.int32, (8, 128), 0)
    odd = jnp.full((8, 128), col % 2, jnp.int32) == 1
    for copy in copies:
        copy.wait()
    for half in range(2):
        sides = []
        for comp in range(COMPS):
            eight = forces_ref[comp, :, pl.ds(128 * half, 128)]
            sides.append(jnp.where(odd, pltpu.roll(eight, 4, axis=0), eight))
        place = jnp.concatenate(
            [particles_ref[:, pl.ds(128 * half, 128)], jnp.zeros((5, 128), jnp.float32)], axis=0
        )
        listed = jnp.full((8, 128), -1.0, jnp.float32)
        for entry in range(4):
            name = jnp.full((8, 128), neighbours_ref[half, entry], jnp.int32).astype(jnp.float32)
            listed = jnp.where(lane == 96 + entry, name, listed)
        for quarter in range(4):
            value = None
            for at, piece in enumerate([*sides, place]):
                turn = (SLICE * (at - quarter)) % 128
                piece = pltpu.roll(piece, turn, axis=1) if turn else piece
                value = piece if value is None else jnp.where(lane >= SLICE * at, piece, value)
            value = jnp.where((lane >= 96) & (line == 3), listed, value)
            sent[4 * half + quarter] = value[0:4]
    copies = [pltpu.make_async_copy(sent, out_hbm.at[row], wrote.at[row]) for row in range(ROWS)]
    for copy in copies:
        copy.start()
    for copy in copies:
        copy.wait()


def payload(forces, particles, neighbours):
    return pl.pallas_call(
        payload_kernel,
        out_shape=pltpu.HBM((ROWS, COLS, SHARE, 128), jnp.float32),
        in_specs=[IN_PLACE] * 3,
        out_specs=IN_PLACE,
        scratch_shapes=[
            pltpu.VMEM((COMPS, 8, 256), jnp.float32),
            pltpu.VMEM((COMPS, 256), jnp.float32),
            pltpu.SMEM((2, 4), jnp.int32),
            pltpu.VMEM((COLS, SHARE, 128), jnp.float32),
            pltpu.SemaphoreType.DMA((3,)),
            pltpu.SemaphoreType.DMA((ROWS,)),
        ],
        name="payload",
        compiler_params=GRANT,
    )(stay(forces), stay(particles), stay(neighbours))


def prepare_kernel(factor_ref, inverses_ref, carried_ref, fh_ref, fl_ref, lend_ref, ih_ref, il_ref, mine_ref):
    for panel in range(2):
        for comp in range(COMPS):
            for block in range(BLOCKS_DEV):
                rows = pl.ds(BLOCKS_DEV * comp + block, COLUMNS, stride=COMPS * BLOCKS_DEV)
                value = factor_ref[panel, rows, :]
                high, low = halves(value)
                pair = 2 * comp + block // 2
                lanes = pl.ds(128 * (block % 2), 128)
                fh_ref[panel, pair, :, lanes] = high
                fl_ref[panel, pair, :, lanes] = low
                if panel == 0 and comp == 1 and block == 0:
                    for quarter in range(4):
                        lend_ref[quarter] = value[128 * quarter : 128 * quarter + 128]
    for quarter in range(4):
        lend_ref[4 + quarter] = inverses_ref[1, :, pl.ds(128 * quarter, 128)]
    high, low = halves(inverses_ref[0])
    ih_ref[...] = high
    il_ref[...] = low
    owner = lax.broadcasted_iota(jnp.int32, (RHS, 128), 0) // SHARE
    own = owner == jnp.full((RHS, 128), lax.axis_index("col"), jnp.int32)
    for block in range(BLOCKS_DEV):
        for comp in range(COMPS):
            mine_ref[block, comp] = jnp.where(own, carried_ref[block, comp], 0.0)


def prepare(factor_rows, inverses, carried):
    panels = (2, 2 * COMPS, COLUMNS, 256)
    return pl.pallas_call(
        prepare_kernel,
        out_shape=(
            pltpu.HBM(panels, jnp.bfloat16),
            pltpu.HBM(panels, jnp.bfloat16),
            pltpu.HBM((8, 128, 128), jnp.float32),
            kept((128, COLUMNS), jnp.bfloat16),
            kept((128, COLUMNS), jnp.bfloat16),
            kept(carried.shape),
        ),
        in_specs=[ON_CHIP] * 3,
        out_specs=(ON_CHIP,) * 6,
        name="prepare",
        compiler_params=GRANT,
    )(factor_rows, inverses, carried)


def fill(places_ref, source):
    for comp in range(COMPS):
        for group in range(ROWS):
            column = places_ref[comp, :, group : group + 1]
            source[comp, pl.ds(SLICE * group, SLICE), :] = jnp.broadcast_to(column, (SLICE, 128))


def couple(blocks, points_ref, flags_ref, push_ref, source_ref, high, low):
    width = 128 * len(blocks)
    totals = [None] * COMPS
    for tile in range(4):
        slot = tile % 2
        for where, block in enumerate(blocks):
            lanes = pl.ds(128 * where, 128)
            points = [points_ref[c : c + 1, pl.ds(128 * block, 128)] for c in range(COMPS)]
            flags = flags_ref[block : block + 1, :]
            for at in range(8):
                group = 8 * tile + at
                rows = pl.ds(SLICE * at, SLICE)
                spots = pl.ds(SLICE * group, SLICE)
                diff = [points[c] - source_ref[c, spots, :] for c in range(COMPS)]
                flag = jnp.broadcast_to(flags[:, 8 * group : 8 * group + 1], (SLICE, 128))
                radius = diff[0] * diff[0] + diff[1] * diff[1] + diff[2] * diff[2] + 1.0
                root = lax.rsqrt(radius)
                cube = root * root * root * flag
                iso = (radius + 1.0) * cube
                scaled = [diff[0] * cube, diff[1] * cube, diff[2] * cube]
                for n, (a, b) in enumerate(PAIRS):
                    value = scaled[a] * diff[b]
                    top, rest = halves(value + iso if a == b else value)
                    high[slot, n, rows, lanes] = top
                    low[slot, n, rows, lanes] = rest
        for n, (a, b) in enumerate(PAIRS):
            if a == b:
                left, first = push_ref[b, tile], push_ref[b, tile, 0:32]
            else:
                left = jnp.concatenate([push_ref[b, tile], push_ref[a, tile]], axis=0)
                first = jnp.concatenate(
                    [push_ref[b, tile, 0:32], push_ref[a, tile, 0:32]], axis=0
                )
            full = jnp.dot(left, high[slot, n, :, 0:width], preferred_element_type=jnp.float32)
            rest = jnp.dot(first, low[slot, n, :, 0:width], preferred_element_type=jnp.float32)
            add = full[0:32] + full[32:64] + rest[0:32]
            totals[a] = add if totals[a] is None else totals[a] + add
            if a != b:
                add = full[64:96] + full[96:128] + rest[32:64]
                totals[b] = add if totals[b] is None else totals[b] + add
    return totals


def near_first_kernel(
    got_ref, points_ref, mine_ref, out_ref, spread_ref, push_ref, places_ref, flags_ref, source_ref, high, low
):
    lane = lax.broadcasted_iota(jnp.int32, (RHS, 128), 1) // SLICE
    for quad in range(8):
        for comp in range(COMPS):
            joined = None
            for at in range(4):
                piece = got_ref[pl.ds(RHS * (4 * quad + at), RHS), :]
                turn = (SLICE * (at - comp)) % 128
                piece = pltpu.roll(piece, turn, axis=1) if turn else piece
                joined = piece if joined is None else jnp.where(lane == at, piece, joined)
            top, rest = halves(joined)
            lanes = pl.ds(128 * (quad % 2), 128)
            push_ref[comp, quad // 2, 0:32, lanes] = top
            push_ref[comp, quad // 2, 32:64, lanes] = rest
    for comp in range(COMPS):
        places_ref[comp] = got_ref[pl.ds(comp, ROWS, stride=RHS), :].T[96:128, :]
    fill(places_ref, source_ref)
    lists = got_ref[pl.ds(3, ROWS * COLS, stride=4), :].T[96:104, :]
    first = BLOCKS_DEV * lax.axis_index("row")
    for block in range(BLOCKS_DEV):
        name = jnp.full(lists.shape, first + block, jnp.int32).astype(jnp.float32)
        found = jnp.where(lists == name, 1.0, 0.0)
        for step in (1, 2, 4):
            found = jnp.maximum(found, pltpu.roll(found, ROWS * COLS - step, axis=1))
        flags_ref[block : block + 1, :] = jnp.max(found, axis=0, keepdims=True)
    totals = couple((0,), points_ref, flags_ref, push_ref, source_ref, high, low)
    for comp in range(COMPS):
        value = totals[comp] + mine_ref[0, comp]
        out_ref[comp] = value
        if comp == 0:
            for part in range(COLS):
                spread_ref[part] = value


def near_first(got, points, mine):
    return pl.pallas_call(
        near_first_kernel,
        out_shape=(
            kept((COMPS, RHS, 128)),
            kept((COLS, RHS, 128)),
            kept((COMPS, 4, 64, 256), jnp.bfloat16),
            kept((COMPS, SLICE, ROWS)),
            kept((BLOCKS_DEV, 256)),
        ),
        in_specs=[ON_CHIP] * 3,
        out_specs=(ON_CHIP,) * 5,
        scratch_shapes=[pltpu.VMEM((COMPS, ROWS * SLICE, 128), jnp.float32)]
        + [pltpu.VMEM((2, 6, 256, 128), jnp.bfloat16)] * 2,
        name="near_first",
        compiler_params=GRANT,
    )(keep(got), points, keep(mine))


def near_rest_kernel(
    points_ref, mine_ref, push_ref, places_ref, flags_ref, out_ref, source_ref, high, low
):
    fill(places_ref, source_ref)
    for blocks in ((1, 2), (3,)):
        totals = couple(blocks, points_ref, flags_ref, push_ref, source_ref, high, low)
        for where, block in enumerate(blocks):
            for comp in range(COMPS):
                value = totals[comp][:, 128 * where : 128 * where + 128]
                out_ref[block - 1, comp] = value + mine_ref[block, comp]


def near_rest(points, mine, push, places, flags):
    return pl.pallas_call(
        near_rest_kernel,
        out_shape=kept((BLOCKS_DEV - 1, COMPS, RHS, 128)),
        in_specs=[ON_CHIP] * 5,
        out_specs=ON_CHIP,
        scratch_shapes=[pltpu.VMEM((COMPS, ROWS * SLICE, 128), jnp.float32)]
        + [pltpu.VMEM((2, 6, 256, 256), jnp.bfloat16)] * 2,
        name="near_rest",
        compiler_params=GRANT,
    )(points, keep(mine), keep(push), keep(places), keep(flags))


def total(parts_ref):
    value = parts_ref[0]
    for part in range(1, parts_ref.shape[0]):
        value = value + parts_ref[part]
    return value


def first_solve_kernel(parts_ref, ih_ref, il_ref, near_ref, out_ref):
    value = product(total(parts_ref), ih_ref[...], il_ref[...])
    for y in range(RING):
        sides = slice(EIGHT * y, EIGHT * y + EIGHT)
        for quarter in range(4):
            out_ref[y, pl.ds(EIGHT * quarter, EIGHT), :] = value[sides, 128 * quarter : 128 * quarter + 128]
        out_ref[y, pl.ds(32, EIGHT), :] = near_ref[1, pl.ds(EIGHT * y, EIGHT), :]


def first_solve(parts, ih, il, near):
    return pl.pallas_call(
        first_solve_kernel,
        out_shape=kept((RING, 40, 128)),
        in_specs=[ON_CHIP] * 4,
        out_specs=ON_CHIP,
        name="first_solve",
        compiler_params=GRANT,
    )(keep(parts), keep(ih), keep(il), keep(near))


def add_kernel(got_ref, out_ref):
    value = total(got_ref)[0:32]
    for part in range(DEPTH):
        out_ref[part] = value


def add(got):
    return pl.pallas_call(
        add_kernel,
        out_shape=kept((DEPTH, 32, 128)),
        in_specs=[ON_CHIP],
        out_specs=ON_CHIP,
        name="add",
        compiler_params=GRANT,
    )(keep(got))


def wide(value):
    return jnp.concatenate([value[EIGHT * q : EIGHT * q + EIGHT] for q in range(4)], axis=1)


def diagonal_kernel(parts_ref, got_ref, own_ref, one_ref, two_ref, three_ref, answer_ref, out_ref):
    value = total(parts_ref)
    answer_ref[...] = value
    answer = wide(value)
    y = lax.axis_index("row") % RING
    for step, tiles in enumerate((own_ref, one_ref, two_ref, three_ref)):
        columns = jnp.concatenate([tiles[quarter] for quarter in range(4)], axis=0)
        base = got_ref[(y + step) % RING, pl.ds(32, EIGHT), :]
        value = base - product(answer, *halves(columns))
        for part in range(COLS):
            out_ref[part, pl.ds(EIGHT * step, EIGHT), :] = value


def diagonal(parts, got, tiles):
    return pl.pallas_call(
        diagonal_kernel,
        out_shape=(kept((32, 128)), kept((COLS, 32, 128))),
        in_specs=[ON_CHIP] * 6,
        out_specs=(ON_CHIP,) * 2,
        name="diagonal",
        compiler_params=GRANT,
    )(keep(parts), keep(got), *[keep(tile) for tile in tiles])


def second_solve_kernel(parts_ref, own_ref, one_ref, two_ref, three_ref, out_ref):
    diag = total(parts_ref)
    value = None
    for step, tiles in enumerate((own_ref, one_ref, two_ref, three_ref)):
        inverse = jnp.concatenate([tiles[4 + quarter] for quarter in range(4)], axis=1)
        add = product(diag[EIGHT * step : EIGHT * step + EIGHT], *halves(inverse))
        value = add if value is None else value + add
    for part in range(DEPTH):
        for quarter in range(4):
            out_ref[part, pl.ds(EIGHT * quarter, EIGHT), :] = value[:, 128 * quarter : 128 * quarter + 128]


def second_solve(parts, tiles):
    return pl.pallas_call(
        second_solve_kernel,
        out_shape=kept((DEPTH, 32, 128)),
        in_specs=[ON_CHIP] * 5,
        out_specs=ON_CHIP,
        name="second_solve",
        compiler_params=GRANT,
    )(keep(parts), *[keep(tile) for tile in tiles])


def gather_kernel(parts_ref, first_ref, out_ref):
    second = total(parts_ref)
    for y in range(RING):
        out_ref[y, 0:32] = first_ref[...]
        out_ref[y, 32:64] = second


def gather(parts, first):
    return pl.pallas_call(
        gather_kernel,
        out_shape=kept((RING, 64, 128)),
        in_specs=[ON_CHIP] * 2,
        out_specs=ON_CHIP,
        name="gather",
        compiler_params=GRANT,
    )(keep(parts), keep(first))


def whole(got_ref, panel):
    columns = []
    for quarter in range(4):
        rows = pl.ds(32 * panel + EIGHT * quarter, EIGHT)
        columns.append(jnp.concatenate([got_ref[y, rows, :] for y in range(RING)], axis=0))
    return jnp.concatenate(columns, axis=1)


def answers_kernel(got_ref, out_ref):
    for panel in range(2):
        out_ref[panel] = whole(got_ref, panel)


def answers(got):
    return pl.pallas_call(
        answers_kernel,
        out_shape=jax.ShapeDtypeStruct((2, RHS, COLUMNS), jnp.float32),
        in_specs=[ON_CHIP],
        out_specs=ON_CHIP,
        name="answers",
        compiler_params=GRANT,
    )(keep(got))


def change_kernel(got_ref, fh_hbm, fl_hbm, first_ref, rest_ref, out_ref, high, low, read):
    count = 4 * COMPS
    copies = []
    for at in range(count):
        panel, pair = at % 2, at // 2
        copies.append(pltpu.make_async_copy(fh_hbm.at[panel, pair], high.at[at], read.at[at]))
        copies.append(pltpu.make_async_copy(fl_hbm.at[panel, pair], low.at[at], read.at[count + at]))
    for copy in copies:
        copy.start()
    sides = [whole(got_ref, panel) for panel in range(2)]
    for comp in range(COMPS):
        for pair in range(2):
            moved = []
            for panel in range(2):
                at = 2 * (2 * comp + pair) + panel
                copies[2 * at].wait()
                copies[2 * at + 1].wait()
                moved.append(product(sides[panel], high[at], low[at]))
            for where in range(2):
                block = 2 * pair + where
                value = first_ref[comp] if block == 0 else rest_ref[block - 1, comp]
                for panel in range(2):
                    if block > 0 or comp > panel:
                        value = value - moved[panel][:, 128 * where : 128 * where + 128]
                for part in range(COLS):
                    out_ref[part, block, comp] = value[SHARE * part : SHARE * part + SHARE]


def change(got, fh, fl, first, rest):
    return pl.pallas_call(
        change_kernel,
        out_shape=pltpu.HBM((COLS, BLOCKS_DEV, COMPS, SHARE, 128), jnp.float32),
        in_specs=[ON_CHIP, IN_PLACE, IN_PLACE, ON_CHIP, ON_CHIP],
        out_specs=ON_CHIP,
        scratch_shapes=[
            pltpu.VMEM((4 * COMPS, COLUMNS, 256), jnp.bfloat16),
            pltpu.VMEM((4 * COMPS, COLUMNS, 256), jnp.bfloat16),
            pltpu.SemaphoreType.DMA((8 * COMPS,)),
        ],
        name="change",
        compiler_params=GRANT,
    )(keep(got), stay(fh), stay(fl), keep(first), keep(rest))


def along(array, groups):
    return lax.all_to_all(array, "row", 0, 0, axis_index_groups=groups, tiled=True)


def body(obstacles, particles, forces, neighbours, carried, factor, inverses):
    ring = [[RING * z + y for y in range(RING)] for z in range(DEPTH)]
    line = [[RING * z + y for z in range(DEPTH)] for y in range(RING)]
    sent = payload(forces, particles, neighbours).reshape(ROWS * COLS, SHARE, 128)
    got = lax.all_to_all(sent, ("row", "col"), 0, 0, tiled=True).reshape(ROWS * RHS, 128)
    rows = factor.transpose(0, 1, 3, 2, 4).reshape(2, COLUMNS * COMPS * BLOCKS_DEV, 128)
    fh, fl, lend, ih, il, mine = prepare(rows, inverses, carried)
    tiles = [lend]
    for step in range(1, RING):
        pairs = [(RING * z + (y + step) % RING, RING * z + y) for z in range(DEPTH) for y in range(RING)]
        tiles.append(lax.ppermute(lend, "row", pairs))
    near0, spread, push, places, flags = near_first(got, obstacles, mine)
    parts = lax.all_to_all(spread, "col", 0, 0, tiled=True)
    rest = near_rest(obstacles, mine, push, places, flags)
    shares = along(first_solve(parts, ih, il, near0), ring)
    parts = along(add(shares), line)
    parts, rest = lax.optimization_barrier((parts, rest))
    first, spread = diagonal(parts, shares, tiles)
    parts = lax.all_to_all(spread, "col", 0, 0, tiled=True)
    parts = along(second_solve(parts, tiles), line)
    shares = along(gather(parts, first), ring)
    back = lax.all_to_all(change(shares, fh, fl, near0, rest), "col", 0, 0, tiled=True)
    return (answers(shares), jnp.sum(back, axis=0))


def solution(mesh):
    in_specs = (
        P(None, "row"),
        P(None, "row"),
        P(None, None, "row"),
        P("row", "col"),
        P("row", None, None, None),
        P(None, "col", "row", None, None),
        P(None, "row", "col"),
    )
    out_specs = (P(None, None, "col"), P("row", None, "col", None))
    return jax.shard_map(body, mesh=mesh, in_specs=in_specs, out_specs=out_specs, check_vma=False)
```

```python
import jax
import jax.numpy as jnp
from jax import lax
from jax.experimental import pallas as pl
from jax.experimental.pallas import tpu as pltpu
from jax.sharding import PartitionSpec as P


ROWS = 32
COLS = 8
BLOCKS_DEV = 4
SLICE = 32
RHS = 32
COMPS = 3
PAIRS = ((0, 0), (1, 1), (2, 2), (0, 1), (0, 2), (1, 2))
SHARE = RHS // COLS
COLUMNS = 512
RING = 4
DEPTH = 8
EIGHT = RHS // RING


ON_CHIP = pl.BlockSpec(memory_space=pltpu.VMEM)
IN_PLACE = pl.BlockSpec(memory_space=pltpu.HBM)
GRANT = pltpu.CompilerParams(vmem_limit_bytes=16 << 20)


def kept(shape, dtype=jnp.float32):
    return pltpu.VMEM(shape, dtype)


def keep(array):
    return pltpu.with_memory_space_constraint(array, pltpu.VMEM)


def stay(array):
    return pltpu.with_memory_space_constraint(array, pltpu.HBM)


def halves(value):
    high = value.astype(jnp.bfloat16)
    return high, (value - high.astype(jnp.float32)).astype(jnp.bfloat16)


def product(left, high, low):
    top, rest = halves(left)
    both = jnp.concatenate([top, rest], axis=0)
    full = jnp.dot(both, high, preferred_element_type=jnp.float32)
    part = jnp.dot(top, low, preferred_element_type=jnp.float32)
    count = left.shape[0]
    return full[:count] + full[count:] + part


def payload_kernel(
    forces_hbm, particles_hbm, neighbours_hbm, out_hbm, forces_ref, particles_ref, neighbours_ref, sent, read, wrote
):
    col = lax.axis_index("col")
    start = pl.multiple_of((col // 2) * 8, 8)
    copies = [
        pltpu.make_async_copy(forces_hbm.at[:, pl.ds(start, 8), :], forces_ref, read.at[0]),
        pltpu.make_async_copy(particles_hbm, particles_ref, read.at[1]),
        pltpu.make_async_copy(neighbours_hbm, neighbours_ref, read.at[2]),
    ]
    for copy in copies:
        copy.start()
    lane = lax.broadcasted_iota(jnp.int32, (8, 128), 1)
    line = lax.broadcasted_iota(jnp.int32, (8, 128), 0)
    odd = jnp.full((8, 128), col % 2, jnp.int32) == 1
    for copy in copies:
        copy.wait()
    for half in range(2):
        sides = []
        for comp in range(COMPS):
            eight = forces_ref[comp, :, pl.ds(128 * half, 128)]
            sides.append(jnp.where(odd, pltpu.roll(eight, 4, axis=0), eight))
        place = jnp.concatenate(
            [particles_ref[:, pl.ds(128 * half, 128)], jnp.zeros((5, 128), jnp.float32)], axis=0
        )
        listed = jnp.full((8, 128), -1.0, jnp.float32)
        for entry in range(4):
            name = jnp.full((8, 128), neighbours_ref[half, entry], jnp.int32).astype(jnp.float32)
            listed = jnp.where(lane == 96 + entry, name, listed)
        for quarter in range(4):
            value = None
            for at, piece in enumerate([*sides, place]):
                turn = (SLICE * (at - quarter)) % 128
                piece = pltpu.roll(piece, turn, axis=1) if turn else piece
                value = piece if value is None else jnp.where(lane >= SLICE * at, piece, value)
            value = jnp.where((lane >= 96) & (line == 3), listed, value)
            sent[4 * half + quarter] = value[0:4]
    copies = [pltpu.make_async_copy(sent, out_hbm.at[row], wrote.at[row]) for row in range(ROWS)]
    for copy in copies:
        copy.start()
    for copy in copies:
        copy.wait()


def payload(forces, particles, neighbours):
    return pl.pallas_call(
        payload_kernel,
        out_shape=pltpu.HBM((ROWS, COLS, SHARE, 128), jnp.float32),
        in_specs=[IN_PLACE] * 3,
        out_specs=IN_PLACE,
        scratch_shapes=[
            pltpu.VMEM((COMPS, 8, 256), jnp.float32),
            pltpu.VMEM((COMPS, 256), jnp.float32),
            pltpu.SMEM((2, 4), jnp.int32),
            pltpu.VMEM((COLS, SHARE, 128), jnp.float32),
            pltpu.SemaphoreType.DMA((3,)),
            pltpu.SemaphoreType.DMA((ROWS,)),
        ],
        name="payload",
        compiler_params=GRANT,
    )(stay(forces), stay(particles), stay(neighbours))


def lend_kernel(inverses_hbm, out_hbm, done):
    copy = pltpu.make_async_copy(inverses_hbm.at[0], out_hbm, done)
    copy.start()
    copy.wait()


def lend(inverses):
    return pl.pallas_call(
        lend_kernel,
        out_shape=pltpu.HBM(inverses.shape[1:], jnp.float32),
        in_specs=[IN_PLACE],
        out_specs=IN_PLACE,
        scratch_shapes=[pltpu.SemaphoreType.DMA],
        name="lend",
        compiler_params=GRANT,
    )(stay(inverses))


def prepare_kernel(factor_ref, inverses_ref, carried_ref, _, fh_ref, fl_ref, late_ref, mine_ref):
    for panel in range(2):
        for comp in range(COMPS):
            for block in range(BLOCKS_DEV):
                rows = pl.ds(BLOCKS_DEV * comp + block, COLUMNS, stride=COMPS * BLOCKS_DEV)
                value = factor_ref[panel, rows, :]
                high, low = halves(value)
                pair = 2 * comp + block // 2
                lanes = pl.ds(128 * (block % 2), 128)
                fh_ref[panel, pair, :, lanes] = high
                fl_ref[panel, pair, :, lanes] = low
                if panel == 0 and comp == 1 and block == 0:
                    for quarter in range(4):
                        late_ref[quarter] = value[128 * quarter : 128 * quarter + 128]
    for quarter in range(4):
        lanes = pl.ds(128 * quarter, 128)
        late_ref[4 + quarter] = inverses_ref[1, :, lanes]
    owner = lax.broadcasted_iota(jnp.int32, (RHS, 128), 0) // SHARE
    own = owner == jnp.full((RHS, 128), lax.axis_index("col"), jnp.int32)
    for block in range(BLOCKS_DEV):
        for comp in range(COMPS):
            mine_ref[block, comp] = jnp.where(own, carried_ref[block, comp], 0.0)


def prepare(factor_rows, inverses, carried, early):
    panels = (2, 2 * COMPS, COLUMNS, 256)
    return pl.pallas_call(
        prepare_kernel,
        out_shape=(
            pltpu.HBM(panels, jnp.bfloat16),
            pltpu.HBM(panels, jnp.bfloat16),
            pltpu.HBM((8, 128, 128), jnp.float32),
            kept(carried.shape),
        ),
        in_specs=[ON_CHIP] * 3 + [IN_PLACE],
        out_specs=(ON_CHIP,) * 4,
        name="prepare",
        compiler_params=GRANT,
    )(factor_rows, inverses, carried, stay(early))


def fill(places_ref, source):
    for comp in range(COMPS):
        for group in range(ROWS):
            column = places_ref[comp, :, group : group + 1]
            source[comp, pl.ds(SLICE * group, SLICE), :] = jnp.broadcast_to(column, (SLICE, 128))


def couple(blocks, points_ref, flags_ref, push_ref, source_ref, high, low):
    width = 128 * len(blocks)
    totals = [None] * COMPS
    for tile in range(4):
        slot = tile % 2
        for where, block in enumerate(blocks):
            lanes = pl.ds(128 * where, 128)
            points = [points_ref[c : c + 1, pl.ds(128 * block, 128)] for c in range(COMPS)]
            flags = flags_ref[block : block + 1, :]
            for at in range(8):
                group = 8 * tile + at
                rows = pl.ds(SLICE * at, SLICE)
                spots = pl.ds(SLICE * group, SLICE)
                diff = [points[c] - source_ref[c, spots, :] for c in range(COMPS)]
                flag = jnp.broadcast_to(flags[:, 8 * group : 8 * group + 1], (SLICE, 128))
                radius = diff[0] * diff[0] + diff[1] * diff[1] + diff[2] * diff[2] + 1.0
                root = lax.rsqrt(radius)
                cube = root * root * root * flag
                iso = (radius + 1.0) * cube
                scaled = [diff[0] * cube, diff[1] * cube, diff[2] * cube]
                for n, (a, b) in enumerate(PAIRS):
                    value = scaled[a] * diff[b]
                    top, rest = halves(value + iso if a == b else value)
                    high[slot, n, rows, lanes] = top
                    low[slot, n, rows, lanes] = rest
        for n, (a, b) in enumerate(PAIRS):
            if a == b:
                left, first = push_ref[b, tile], push_ref[b, tile, 0:32]
            else:
                left = jnp.concatenate([push_ref[b, tile], push_ref[a, tile]], axis=0)
                first = jnp.concatenate(
                    [push_ref[b, tile, 0:32], push_ref[a, tile, 0:32]], axis=0
                )
            full = jnp.dot(left, high[slot, n, :, 0:width], preferred_element_type=jnp.float32)
            rest = jnp.dot(first, low[slot, n, :, 0:width], preferred_element_type=jnp.float32)
            add = full[0:32] + full[32:64] + rest[0:32]
            totals[a] = add if totals[a] is None else totals[a] + add
            if a != b:
                add = full[64:96] + full[96:128] + rest[32:64]
                totals[b] = add if totals[b] is None else totals[b] + add
    return totals


def near_first_kernel(
    got_ref, points_ref, mine_ref, out_ref, spread_ref, push_ref, places_ref, flags_ref, source_ref, high, low
):
    lane = lax.broadcasted_iota(jnp.int32, (RHS, 128), 1) // SLICE
    for quad in range(8):
        for comp in range(COMPS):
            joined = None
            for at in range(4):
                piece = got_ref[pl.ds(RHS * (4 * quad + at), RHS), :]
                turn = (SLICE * (at - comp)) % 128
                piece = pltpu.roll(piece, turn, axis=1) if turn else piece
                joined = piece if joined is None else jnp.where(lane == at, piece, joined)
            top, rest = halves(joined)
            lanes = pl.ds(128 * (quad % 2), 128)
            push_ref[comp, quad // 2, 0:32, lanes] = top
            push_ref[comp, quad // 2, 32:64, lanes] = rest
    for comp in range(COMPS):
        places_ref[comp] = got_ref[pl.ds(comp, ROWS, stride=RHS), :].T[96:128, :]
    fill(places_ref, source_ref)
    lists = got_ref[pl.ds(3, ROWS * COLS, stride=4), :].T[96:104, :]
    first = BLOCKS_DEV * lax.axis_index("row")
    for block in range(BLOCKS_DEV):
        name = jnp.full(lists.shape, first + block, jnp.int32).astype(jnp.float32)
        found = jnp.where(lists == name, 1.0, 0.0)
        for step in (1, 2, 4):
            found = jnp.maximum(found, pltpu.roll(found, ROWS * COLS - step, axis=1))
        flags_ref[block : block + 1, :] = jnp.max(found, axis=0, keepdims=True)
    totals = couple((0,), points_ref, flags_ref, push_ref, source_ref, high, low)
    for comp in range(COMPS):
        value = totals[comp] + mine_ref[0, comp]
        out_ref[comp] = value
        if comp < 2:
            for part in range(RING * COLS):
                y = part // COLS
                spread_ref[part, pl.ds(EIGHT * comp, EIGHT), :] = value[EIGHT * y : EIGHT * y + EIGHT]


def near_first(got, points, mine):
    return pl.pallas_call(
        near_first_kernel,
        out_shape=(
            kept((COMPS, RHS, 128)),
            pltpu.HBM((RING * COLS, 2 * EIGHT, 128), jnp.float32),
            pltpu.HBM((COMPS, 4, 64, 256), jnp.bfloat16),
            pltpu.HBM((COMPS, SLICE, ROWS), jnp.float32),
            pltpu.HBM((BLOCKS_DEV, 256), jnp.float32),
        ),
        in_specs=[ON_CHIP] * 3,
        out_specs=(ON_CHIP,) * 5,
        scratch_shapes=[pltpu.VMEM((COMPS, ROWS * SLICE, 128), jnp.float32)]
        + [pltpu.VMEM((2, 6, 256, 128), jnp.bfloat16)] * 2,
        name="near_first",
        compiler_params=GRANT,
    )(keep(got), points, keep(mine))


def near_rest_kernel(
    points_ref, mine_ref, push_ref, places_ref, flags_ref, out_ref, source_ref, high, low
):
    fill(places_ref, source_ref)
    for blocks in ((1, 2), (3,)):
        totals = couple(blocks, points_ref, flags_ref, push_ref, source_ref, high, low)
        for where, block in enumerate(blocks):
            for comp in range(COMPS):
                value = totals[comp][:, 128 * where : 128 * where + 128]
                out_ref[block - 1, comp] = value + mine_ref[block, comp]


def near_rest(points, mine, push, places, flags):
    return pl.pallas_call(
        near_rest_kernel,
        out_shape=kept((BLOCKS_DEV - 1, COMPS, RHS, 128)),
        in_specs=[ON_CHIP] * 5,
        out_specs=ON_CHIP,
        scratch_shapes=[pltpu.VMEM((COMPS, ROWS * SLICE, 128), jnp.float32)]
        + [pltpu.VMEM((2, 6, 256, 256), jnp.bfloat16)] * 2,
        name="near_rest",
        compiler_params=GRANT,
    )(points, keep(mine), stay(push), stay(places), stay(flags))


def total(parts_ref):
    value = parts_ref[0]
    for part in range(1, parts_ref.shape[0]):
        value = value + parts_ref[part]
    return value


def first_solve_kernel(parts_ref, own_ref, one_ref, two_ref, three_ref, out_ref, base_ref):
    ring_at = lax.axis_index("row") % RING
    for y in range(RING):
        value = parts_ref[COLS * y]
        for part in range(1, COLS):
            value = value + parts_ref[COLS * y + part]
        base_ref[y] = value
    value = None
    for step, tiles in enumerate((own_ref, one_ref, two_ref, three_ref)):
        diag = base_ref[(ring_at + step) % RING, pl.ds(0, EIGHT), :]
        add = product(diag, *halves(tiles[...]))
        value = add if value is None else value + add
    for part in range(DEPTH):
        for quarter in range(4):
            out_ref[part, pl.ds(EIGHT * quarter, EIGHT), :] = value[:, 128 * quarter : 128 * quarter + 128]


def first_solve(parts, tiles):
    return pl.pallas_call(
        first_solve_kernel,
        out_shape=(kept((DEPTH, 32, 128)), kept((RING, 2 * EIGHT, 128))),
        in_specs=[ON_CHIP] * 5,
        out_specs=(ON_CHIP,) * 2,
        name="first_solve",
        compiler_params=GRANT,
    )(keep(parts), *[keep(tile) for tile in tiles])


def wide(value):
    return jnp.concatenate([value[EIGHT * q : EIGHT * q + EIGHT] for q in range(4)], axis=1)


def diagonal_kernel(parts_ref, own_ref, one_ref, two_ref, three_ref, answer_ref, out_ref):
    value = total(parts_ref)
    answer_ref[...] = value
    answer = wide(value)
    for step, tiles in enumerate((own_ref, one_ref, two_ref, three_ref)):
        columns = jnp.concatenate([tiles[quarter] for quarter in range(4)], axis=0)
        value = product(answer, *halves(columns))
        for part in range(COLS):
            out_ref[part, pl.ds(EIGHT * step, EIGHT), :] = value


def diagonal(parts, tiles):
    return pl.pallas_call(
        diagonal_kernel,
        out_shape=(kept((32, 128)), kept((COLS, 32, 128))),
        in_specs=[ON_CHIP] * 5,
        out_specs=(ON_CHIP,) * 2,
        name="diagonal",
        compiler_params=GRANT,
    )(keep(parts), *[keep(tile) for tile in tiles])


def second_solve_kernel(parts_ref, base_ref, answer_ref, own_ref, one_ref, two_ref, three_ref, out_ref):
    row = lax.axis_index("row")
    change = total(parts_ref)
    value = None
    for step, tiles in enumerate((own_ref, one_ref, two_ref, three_ref)):
        inverse = jnp.concatenate([tiles[4 + quarter] for quarter in range(4)], axis=1)
        base = base_ref[(row % RING + step) % RING, pl.ds(EIGHT, EIGHT), :]
        add = product(base - change[EIGHT * step : EIGHT * step + EIGHT], *halves(inverse))
        value = add if value is None else value + add
    tail = [answer_ref[pl.ds(EIGHT * quarter + row // RING, 1), :] for quarter in range(4)]
    tail = jnp.concatenate([*tail, jnp.zeros((4, 128), jnp.float32)], axis=0)
    for part in range(ROWS):
        for quarter in range(4):
            out_ref[part, pl.ds(EIGHT * quarter, EIGHT), :] = value[:, 128 * quarter : 128 * quarter + 128]
        out_ref[part, pl.ds(32, EIGHT), :] = tail


def second_solve(parts, base, answer, tiles):
    return pl.pallas_call(
        second_solve_kernel,
        out_shape=kept((ROWS, 40, 128)),
        in_specs=[ON_CHIP] * 7,
        out_specs=ON_CHIP,
        name="second_solve",
        compiler_params=GRANT,
    )(keep(parts), keep(base), keep(answer), *[keep(tile) for tile in tiles])


def whole(got_ref):
    first, second = [], []
    sums = []
    for y in range(RING):
        value = got_ref[pl.ds(40 * y, 32), :]
        for z in range(1, DEPTH):
            value = value + got_ref[pl.ds(40 * (RING * z + y), 32), :]
        sums.append(value)
    for quarter in range(4):
        lines = [got_ref[pl.ds(40 * y + 32 + quarter, DEPTH, stride=40 * RING), :] for y in range(RING)]
        first.append(jnp.concatenate(lines, axis=0))
        lines = [value[EIGHT * quarter : EIGHT * quarter + EIGHT] for value in sums]
        second.append(jnp.concatenate(lines, axis=0))
    return jnp.concatenate(first, axis=1), jnp.concatenate(second, axis=1)


def answers_kernel(got_ref, out_ref):
    out_ref[0], out_ref[1] = whole(got_ref)


def answers(got):
    return pl.pallas_call(
        answers_kernel,
        out_shape=jax.ShapeDtypeStruct((2, RHS, COLUMNS), jnp.float32),
        in_specs=[ON_CHIP],
        out_specs=ON_CHIP,
        name="answers",
        compiler_params=GRANT,
    )(keep(got))


def change_kernel(got_ref, fh_hbm, fl_hbm, first_ref, rest_ref, out_ref, high, low, read):
    count = 4 * COMPS
    copies = []
    for at in range(count):
        panel, pair = at % 2, at // 2
        copies.append(pltpu.make_async_copy(fh_hbm.at[panel, pair], high.at[at], read.at[at]))
        copies.append(pltpu.make_async_copy(fl_hbm.at[panel, pair], low.at[at], read.at[count + at]))
    for copy in copies:
        copy.start()
    sides = whole(got_ref)
    for comp in range(COMPS):
        for pair in range(2):
            moved = []
            for panel in range(2):
                at = 2 * (2 * comp + pair) + panel
                copies[2 * at].wait()
                copies[2 * at + 1].wait()
                moved.append(product(sides[panel], high[at], low[at]))
            for where in range(2):
                block = 2 * pair + where
                value = first_ref[comp] if block == 0 else rest_ref[block - 1, comp]
                for panel in range(2):
                    if block > 0 or comp > panel:
                        value = value - moved[panel][:, 128 * where : 128 * where + 128]
                for part in range(COLS):
                    out_ref[part, block, comp] = value[SHARE * part : SHARE * part + SHARE]


def change(got, fh, fl, first, rest):
    return pl.pallas_call(
        change_kernel,
        out_shape=pltpu.HBM((COLS, BLOCKS_DEV, COMPS, SHARE, 128), jnp.float32),
        in_specs=[ON_CHIP, IN_PLACE, IN_PLACE, ON_CHIP, ON_CHIP],
        out_specs=ON_CHIP,
        scratch_shapes=[
            pltpu.VMEM((4 * COMPS, COLUMNS, 256), jnp.bfloat16),
            pltpu.VMEM((4 * COMPS, COLUMNS, 256), jnp.bfloat16),
            pltpu.SemaphoreType.DMA((8 * COMPS,)),
        ],
        name="change",
        compiler_params=GRANT,
    )(keep(got), stay(fh), stay(fl), keep(first), keep(rest))


def body(obstacles, particles, forces, neighbours, carried, factor, inverses):
    everyone = ("row", "col")
    plane = [[32 * z + at for at in range(RING * COLS)] for z in range(DEPTH)]
    line = [[RING * z + y for z in range(DEPTH)] for y in range(RING)]
    sent = payload(forces, particles, neighbours).reshape(ROWS * COLS, SHARE, 128)
    got = lax.all_to_all(sent, everyone, 0, 0, tiled=True).reshape(ROWS * RHS, 128)
    rows = factor.transpose(0, 1, 3, 2, 4).reshape(2, COLUMNS * COMPS * BLOCKS_DEV, 128)
    early = lend(inverses)
    fh, fl, late, mine = prepare(rows, inverses, carried, early)
    tiles = []
    for lent in (early, late):
        shared = [lent]
        for step in range(1, RING):
            pairs = [
                (RING * z + (y + step) % RING, RING * z + y) for z in range(DEPTH) for y in range(RING)
            ]
            shared.append(lax.ppermute(lent, "row", pairs))
        tiles.append(shared)
    near0, spread, push, places, flags = near_first(got, obstacles, mine)
    parts = lax.all_to_all(stay(spread), everyone, 0, 0, axis_index_groups=plane, tiled=True)
    rest = near_rest(obstacles, mine, push, places, flags)
    parts, rest = lax.optimization_barrier((parts, rest))
    spread, base = first_solve(parts, tiles[0])
    parts = lax.all_to_all(spread, "row", 0, 0, axis_index_groups=line, tiled=True)
    first, spread = diagonal(parts, tiles[1])
    parts = lax.all_to_all(spread, "col", 0, 0, tiled=True)
    spread = second_solve(parts, base, first, tiles[1])
    shares = lax.all_to_all(spread, "row", 0, 0, tiled=True).reshape(ROWS * 40, 128)
    back = lax.all_to_all(change(shares, fh, fl, near0, rest), "col", 0, 0, tiled=True)
    return (answers(shares), jnp.sum(back, axis=0))


def solution(mesh):
    in_specs = (
        P(None, "row"),
        P(None, "row"),
        P(None, None, "row"),
        P("row", "col"),
        P("row", None, None, None),
        P(None, "col", "row", None, None),
        P(None, "row", "col"),
    )
    out_specs = (P(None, None, "col"), P("row", None, "col", None))
    return jax.shard_map(body, mesh=mesh, in_specs=in_specs, out_specs=out_specs, check_vma=False)
```

```python
import functools

import jax
import jax.numpy as jnp
from jax import lax
from jax.experimental import pallas as pl
from jax.experimental.pallas import tpu as pltpu
from jax.sharding import PartitionSpec as P

ROWS = 32
COLS = 8
BLOCKS_DEV = 4
SLICE = 32
RHS = 32
COMPS = 3
PAIRS = ((0, 0), (1, 1), (2, 2), (0, 1), (0, 2), (1, 2))
SHARE = RHS // COLS
COLUMNS = 512
RING = 4
DEPTH = 8
EIGHT = RHS // RING


ON_CHIP = pl.BlockSpec(memory_space=pltpu.VMEM)
IN_PLACE = pl.BlockSpec(memory_space=pltpu.HBM)
GRANT = pltpu.CompilerParams(vmem_limit_bytes=16 << 20)


def kept(shape, dtype=jnp.float32):
    return pltpu.VMEM(shape, dtype)


def keep(array):
    return pltpu.with_memory_space_constraint(array, pltpu.VMEM)


def stay(array):
    return pltpu.with_memory_space_constraint(array, pltpu.HBM)


def halves(value):
    high = value.astype(jnp.bfloat16)
    return high, (value - high.astype(jnp.float32)).astype(jnp.bfloat16)


def product(left, high, low):
    top, rest = halves(left)
    both = jnp.concatenate([top, rest], axis=0)
    full = jnp.dot(both, high, preferred_element_type=jnp.float32)
    part = jnp.dot(top, low, preferred_element_type=jnp.float32)
    count = left.shape[0]
    return full[:count] + full[count:] + part


def payload_kernel(
    forces_hbm, particles_hbm, neighbours_hbm, out_hbm, forces_ref, particles_ref, neighbours_ref, sent, read, wrote
):
    col = lax.axis_index("col")
    start = pl.multiple_of((col // 2) * 8, 8)
    copies = [
        pltpu.make_async_copy(forces_hbm.at[:, pl.ds(start, 8), :], forces_ref, read.at[0]),
        pltpu.make_async_copy(particles_hbm, particles_ref, read.at[1]),
        pltpu.make_async_copy(neighbours_hbm, neighbours_ref, read.at[2]),
    ]
    for copy in copies:
        copy.start()
    lane = lax.broadcasted_iota(jnp.int32, (8, 128), 1)
    line = lax.broadcasted_iota(jnp.int32, (8, 128), 0)
    odd = jnp.full((8, 128), col % 2, jnp.int32) == 1
    for copy in copies:
        copy.wait()
    for half in range(2):
        sides = []
        for comp in range(COMPS):
            eight = forces_ref[comp, :, pl.ds(128 * half, 128)]
            sides.append(jnp.where(odd, pltpu.roll(eight, 4, axis=0), eight))
        place = jnp.concatenate(
            [particles_ref[:, pl.ds(128 * half, 128)], jnp.zeros((5, 128), jnp.float32)], axis=0
        )
        listed = jnp.full((8, 128), -1.0, jnp.float32)
        for entry in range(4):
            name = jnp.full((8, 128), neighbours_ref[half, entry], jnp.int32).astype(jnp.float32)
            listed = jnp.where(lane == 96 + entry, name, listed)
        for quarter in range(4):
            value = None
            for at, piece in enumerate([*sides, place]):
                turn = (SLICE * (at - quarter)) % 128
                piece = pltpu.roll(piece, turn, axis=1) if turn else piece
                value = piece if value is None else jnp.where(lane >= SLICE * at, piece, value)
            value = jnp.where((lane >= 96) & (line == 3), listed, value)
            sent[4 * half + quarter] = value[0:4]
    copies = [pltpu.make_async_copy(sent, out_hbm.at[row], wrote.at[row]) for row in range(ROWS)]
    for copy in copies:
        copy.start()
    for copy in copies:
        copy.wait()


def payload(forces, particles, neighbours):
    return pl.pallas_call(
        payload_kernel,
        out_shape=pltpu.HBM((ROWS, COLS, SHARE, 128), jnp.float32),
        in_specs=[IN_PLACE] * 3,
        out_specs=IN_PLACE,
        scratch_shapes=[
            pltpu.VMEM((COMPS, 8, 256), jnp.float32),
            pltpu.VMEM((COMPS, 256), jnp.float32),
            pltpu.SMEM((2, 4), jnp.int32),
            pltpu.VMEM((COLS, SHARE, 128), jnp.float32),
            pltpu.SemaphoreType.DMA((3,)),
            pltpu.SemaphoreType.DMA((ROWS,)),
        ],
        name="payload",
        compiler_params=GRANT,
    )(stay(forces), stay(particles), stay(neighbours))


def prepare_kernel(
    factor_ref, inverses_ref, carried_ref, fh_ref, fl_ref, lend_ref, ih_ref, il_ref, mine_ref, others_ref
):
    for panel in range(2):
        for comp in range(COMPS):
            for block in range(BLOCKS_DEV):
                rows = pl.ds(BLOCKS_DEV * comp + block, COLUMNS, stride=COMPS * BLOCKS_DEV)
                value = factor_ref[panel, rows, :]
                high, low = halves(value)
                pair = 2 * comp + block // 2
                lanes = pl.ds(128 * (block % 2), 128)
                fh_ref[panel, pair, :, lanes] = high
                fl_ref[panel, pair, :, lanes] = low
                if panel == 0 and comp == 1 and block == 0:
                    for quarter in range(4):
                        lend_ref[quarter] = value[128 * quarter : 128 * quarter + 128]
    for quarter in range(4):
        lend_ref[4 + quarter] = inverses_ref[1, :, pl.ds(128 * quarter, 128)]
    high, low = halves(inverses_ref[0])
    ih_ref[...] = high
    il_ref[...] = low
    owner = lax.broadcasted_iota(jnp.int32, (RHS, 128), 0) // SHARE
    own = owner == jnp.full((RHS, 128), lax.axis_index("col"), jnp.int32)
    for block in range(BLOCKS_DEV):
        for comp in range(COMPS):
            value = jnp.where(own, carried_ref[block, comp], 0.0)
            if block == 0:
                mine_ref[comp] = value
            else:
                others_ref[block - 1, comp] = value


def prepare(factor_rows, inverses, carried):
    panels = (2, 2 * COMPS, COLUMNS, 256)
    return pl.pallas_call(
        prepare_kernel,
        out_shape=(
            pltpu.HBM(panels, jnp.bfloat16),
            pltpu.HBM(panels, jnp.bfloat16),
            kept((8, 128, 128)),
            kept((128, COLUMNS), jnp.bfloat16),
            kept((128, COLUMNS), jnp.bfloat16),
            kept((COMPS, RHS, 128)),
            pltpu.HBM((BLOCKS_DEV - 1, COMPS, RHS, 128), jnp.float32),
        ),
        in_specs=[ON_CHIP] * 3,
        out_specs=(ON_CHIP,) * 7,
        name="prepare",
        compiler_params=GRANT,
    )(factor_rows, inverses, carried)


def fill(places_ref, source):
    for comp in range(COMPS):
        for group in range(ROWS):
            column = places_ref[comp, :, group : group + 1]
            source[comp, pl.ds(SLICE * group, SLICE), :] = jnp.broadcast_to(column, (SLICE, 128))


def couple(blocks, points_ref, flags_ref, push_ref, source_ref, high, low):
    width = 128 * len(blocks)
    totals = [None] * COMPS
    for tile in range(4):
        slot = tile % 2
        for where, block in enumerate(blocks):
            lanes = pl.ds(128 * where, 128)
            points = [points_ref[c : c + 1, pl.ds(128 * block, 128)] for c in range(COMPS)]
            flags = flags_ref[block : block + 1, :]
            for at in range(8):
                group = 8 * tile + at
                rows = pl.ds(SLICE * at, SLICE)
                spots = pl.ds(SLICE * group, SLICE)
                diff = [points[c] - source_ref[c, spots, :] for c in range(COMPS)]
                flag = jnp.broadcast_to(flags[:, 8 * group : 8 * group + 1], (SLICE, 128))
                radius = diff[0] * diff[0] + diff[1] * diff[1] + diff[2] * diff[2] + 1.0
                root = lax.rsqrt(radius)
                cube = root * root * root * flag
                iso = (radius + 1.0) * cube
                scaled = [diff[0] * cube, diff[1] * cube, diff[2] * cube]
                for n, (a, b) in enumerate(PAIRS):
                    value = scaled[a] * diff[b]
                    top, rest = halves(value + iso if a == b else value)
                    high[slot, n, rows, lanes] = top
                    low[slot, n, rows, lanes] = rest
        for n, (a, b) in enumerate(PAIRS):
            if a == b:
                left, first = push_ref[b, tile], push_ref[b, tile, 0:32]
            else:
                left = jnp.concatenate([push_ref[b, tile], push_ref[a, tile]], axis=0)
                first = jnp.concatenate(
                    [push_ref[b, tile, 0:32], push_ref[a, tile, 0:32]], axis=0
                )
            full = jnp.dot(left, high[slot, n, :, 0:width], preferred_element_type=jnp.float32)
            rest = jnp.dot(first, low[slot, n, :, 0:width], preferred_element_type=jnp.float32)
            add = full[0:32] + full[32:64] + rest[0:32]
            totals[a] = add if totals[a] is None else totals[a] + add
            if a != b:
                add = full[64:96] + full[96:128] + rest[32:64]
                totals[b] = add if totals[b] is None else totals[b] + add
    return totals


def near_first_kernel(
    got_ref, points_ref, mine_ref, out_ref, spread_ref, push_ref, places_ref, flags_ref, source_ref, high, low
):
    lane = lax.broadcasted_iota(jnp.int32, (RHS, 128), 1) // SLICE
    for quad in range(8):
        for comp in range(COMPS):
            joined = None
            for at in range(4):
                piece = got_ref[pl.ds(RHS * (4 * quad + at), RHS), :]
                turn = (SLICE * (at - comp)) % 128
                piece = pltpu.roll(piece, turn, axis=1) if turn else piece
                joined = piece if joined is None else jnp.where(lane == at, piece, joined)
            top, rest = halves(joined)
            lanes = pl.ds(128 * (quad % 2), 128)
            push_ref[comp, quad // 2, 0:32, lanes] = top
            push_ref[comp, quad // 2, 32:64, lanes] = rest
    for comp in range(COMPS):
        places_ref[comp] = got_ref[pl.ds(comp, ROWS, stride=RHS), :].T[96:128, :]
    fill(places_ref, source_ref)
    lists = got_ref[pl.ds(3, ROWS * COLS, stride=4), :].T[96:104, :]
    first = BLOCKS_DEV * lax.axis_index("row")
    for block in range(BLOCKS_DEV):
        name = jnp.full(lists.shape, first + block, jnp.int32).astype(jnp.float32)
        found = jnp.where(lists == name, 1.0, 0.0)
        for step in (1, 2, 4):
            found = jnp.maximum(found, pltpu.roll(found, ROWS * COLS - step, axis=1))
        flags_ref[block : block + 1, :] = jnp.max(found, axis=0, keepdims=True)
    totals = couple((0,), points_ref, flags_ref, push_ref, source_ref, high, low)
    for comp in range(COMPS):
        value = totals[comp] + mine_ref[comp]
        out_ref[comp] = value
        if comp == 0:
            for part in range(COLS):
                spread_ref[part] = value


def near_first(got, points, mine):
    return pl.pallas_call(
        near_first_kernel,
        out_shape=(
            kept((COMPS, RHS, 128)),
            kept((COLS, RHS, 128)),
            kept((COMPS, 4, 64, 256), jnp.bfloat16),
            kept((COMPS, SLICE, ROWS)),
            kept((BLOCKS_DEV, 256)),
        ),
        in_specs=[ON_CHIP] * 3,
        out_specs=(ON_CHIP,) * 5,
        scratch_shapes=[pltpu.VMEM((COMPS, ROWS * SLICE, 128), jnp.float32)]
        + [pltpu.VMEM((2, 6, 256, 128), jnp.bfloat16)] * 2,
        name="near_first",
        compiler_params=GRANT,
    )(keep(got), points, keep(mine))


def near_rest_kernel(
    points_ref, push_ref, places_ref, flags_ref, out_ref, source_ref, high, low
):
    fill(places_ref, source_ref)
    for blocks in ((1, 2), (3,)):
        totals = couple(blocks, points_ref, flags_ref, push_ref, source_ref, high, low)
        for where, block in enumerate(blocks):
            for comp in range(COMPS):
                out_ref[block - 1, comp] = totals[comp][:, 128 * where : 128 * where + 128]


def near_rest(points, push, places, flags):
    return pl.pallas_call(
        near_rest_kernel,
        out_shape=kept((BLOCKS_DEV - 1, COMPS, RHS, 128)),
        in_specs=[ON_CHIP] * 4,
        out_specs=ON_CHIP,
        scratch_shapes=[pltpu.VMEM((COMPS, ROWS * SLICE, 128), jnp.float32)]
        + [pltpu.VMEM((2, 6, 256, 256), jnp.bfloat16)] * 2,
        name="near_rest",
        compiler_params=GRANT,
    )(points, keep(push), keep(places), keep(flags))


def total(parts_ref):
    value = parts_ref[0]
    for part in range(1, parts_ref.shape[0]):
        value = value + parts_ref[part]
    return value


def first_solve_kernel(parts_ref, ih_ref, il_ref, near_ref, out_ref):
    value = product(total(parts_ref), ih_ref[...], il_ref[...])
    for y in range(RING):
        sides = slice(EIGHT * y, EIGHT * y + EIGHT)
        for quarter in range(4):
            out_ref[y, pl.ds(EIGHT * quarter, EIGHT), :] = value[sides, 128 * quarter : 128 * quarter + 128]
        out_ref[y, pl.ds(32, EIGHT), :] = near_ref[1, pl.ds(EIGHT * y, EIGHT), :]


def first_solve(parts, ih, il, near):
    return pl.pallas_call(
        first_solve_kernel,
        out_shape=kept((RING, 40, 128)),
        in_specs=[ON_CHIP] * 4,
        out_specs=ON_CHIP,
        name="first_solve",
        compiler_params=GRANT,
    )(keep(parts), keep(ih), keep(il), keep(near))


def add_kernel(got_ref, out_ref):
    value = total(got_ref)[0:32]
    for part in range(DEPTH):
        out_ref[part] = value


def add(got):
    return pl.pallas_call(
        add_kernel,
        out_shape=kept((DEPTH, 32, 128)),
        in_specs=[ON_CHIP],
        out_specs=ON_CHIP,
        name="add",
        compiler_params=GRANT,
    )(keep(got))


def wide(value):
    return jnp.concatenate([value[EIGHT * q : EIGHT * q + EIGHT] for q in range(4)], axis=1)


def diagonal_kernel(parts_ref, got_ref, own_ref, one_ref, two_ref, three_ref, answer_ref, out_ref):
    value = total(parts_ref)
    answer_ref[...] = value
    answer = wide(value)
    y = lax.axis_index("row") % RING
    for step, tiles in enumerate((own_ref, one_ref, two_ref, three_ref)):
        columns = jnp.concatenate([tiles[quarter] for quarter in range(4)], axis=0)
        base = got_ref[(y + step) % RING, pl.ds(32, EIGHT), :]
        value = base - product(answer, *halves(columns))
        for part in range(COLS):
            out_ref[part, pl.ds(EIGHT * step, EIGHT), :] = value


def diagonal(parts, got, tiles):
    return pl.pallas_call(
        diagonal_kernel,
        out_shape=(kept((32, 128)), kept((COLS, 32, 128))),
        in_specs=[ON_CHIP] * 6,
        out_specs=(ON_CHIP,) * 2,
        name="diagonal",
        compiler_params=GRANT,
    )(keep(parts), keep(got), *[keep(tile) for tile in tiles])


def second_solve_kernel(parts_ref, own_ref, one_ref, two_ref, three_ref, out_ref):
    diag = total(parts_ref)
    value = None
    for step, tiles in enumerate((own_ref, one_ref, two_ref, three_ref)):
        inverse = jnp.concatenate([tiles[4 + quarter] for quarter in range(4)], axis=1)
        add = product(diag[EIGHT * step : EIGHT * step + EIGHT], *halves(inverse))
        value = add if value is None else value + add
    for part in range(DEPTH):
        for quarter in range(4):
            out_ref[part, pl.ds(EIGHT * quarter, EIGHT), :] = value[:, 128 * quarter : 128 * quarter + 128]


def second_solve(parts, tiles):
    return pl.pallas_call(
        second_solve_kernel,
        out_shape=kept((DEPTH, 32, 128)),
        in_specs=[ON_CHIP] * 5,
        out_specs=ON_CHIP,
        name="second_solve",
        compiler_params=GRANT,
    )(keep(parts), *[keep(tile) for tile in tiles])


def gather_kernel(parts_ref, first_ref, out_ref):
    second = total(parts_ref)
    for y in range(RING):
        out_ref[y, 0:32] = first_ref[...]
        out_ref[y, 32:64] = second


def gather(parts, first):
    return pl.pallas_call(
        gather_kernel,
        out_shape=kept((RING, 64, 128)),
        in_specs=[ON_CHIP] * 2,
        out_specs=ON_CHIP,
        name="gather",
        compiler_params=GRANT,
    )(keep(parts), keep(first))


def whole(got_ref, panel):
    columns = []
    for quarter in range(4):
        rows = pl.ds(32 * panel + EIGHT * quarter, EIGHT)
        columns.append(jnp.concatenate([got_ref[y, rows, :] for y in range(RING)], axis=0))
    return jnp.concatenate(columns, axis=1)


def change_kernel(
    got_ref, fh_hbm, fl_hbm, others_hbm, first_ref, rest_ref, out_ref, answers_hbm,
    high, low, others, both, read, extra
):
    jobs, copies = [], []
    for comp in range(COMPS):
        for pair in range(2):
            for panel in range(2):
                at = len(jobs)
                hidden = pair == 0 and comp <= panel
                lanes = pl.ds(128, 128) if hidden else pl.ds(0, 256)
                jobs.append((comp, pair, panel, hidden, lanes))
                for side, (source, target) in enumerate(((fh_hbm, high), (fl_hbm, low))):
                    copies.append(
                        pltpu.make_async_copy(
                            source.at[panel, 2 * comp + pair, :, lanes],
                            target.at[at, :, lanes],
                            read.at[2 * at + side],
                        )
                    )
    ahead = 8
    for copy in copies[:ahead]:
        copy.start()
    carry = pltpu.make_async_copy(others_hbm, others, extra.at[0])
    carry.start()
    sides = [whole(got_ref, panel) for panel in range(2)]
    both[0], both[1] = sides
    answer = pltpu.make_async_copy(both, answers_hbm, extra.at[1])
    answer.start()
    moved = [None, None]
    carry.wait()
    for at, (comp, pair, panel, hidden, lanes) in enumerate(jobs):
        for copy in copies[2 * at : 2 * at + 2]:
            copy.wait()
        for copy in copies[2 * at + ahead : 2 * at + ahead + 2]:
            copy.start()
        moved[panel] = product(sides[panel], high[at, :, lanes], low[at, :, lanes])
        if panel == 0:
            continue
        for where in range(2):
            block = 2 * pair + where
            if block == 0:
                value = first_ref[comp]
            else:
                value = rest_ref[block - 1, comp] + others[block - 1, comp]
            for index, part in enumerate(moved):
                if block > 0 or comp > index:
                    start = part.shape[1] - 256 + 128 * where
                    value = value - part[:, start : start + 128]
            for part in range(COLS):
                out_ref[part, block, comp] = value[SHARE * part : SHARE * part + SHARE]
    answer.wait()


def change(got, fh, fl, others, first, rest):
    return pl.pallas_call(
        change_kernel,
        out_shape=(
            kept((COLS, BLOCKS_DEV, COMPS, SHARE, 128)),
            pltpu.HBM((2, RHS, COLUMNS), jnp.float32),
        ),
        in_specs=[ON_CHIP, IN_PLACE, IN_PLACE, IN_PLACE, ON_CHIP, ON_CHIP],
        out_specs=(ON_CHIP, IN_PLACE),
        scratch_shapes=[
            pltpu.VMEM((4 * COMPS, COLUMNS, 256), jnp.bfloat16),
            pltpu.VMEM((4 * COMPS, COLUMNS, 256), jnp.bfloat16),
            pltpu.VMEM((BLOCKS_DEV - 1, COMPS, RHS, 128), jnp.float32),
            pltpu.VMEM((2, RHS, COLUMNS), jnp.float32),
            pltpu.SemaphoreType.DMA((8 * COMPS,)),
            pltpu.SemaphoreType.DMA((2,)),
        ],
        name="change",
        compiler_params=GRANT,
    )(keep(got), stay(fh), stay(fl), stay(others), keep(first), keep(rest))


def along(array, groups):
    return lax.all_to_all(array, "row", 0, 0, axis_index_groups=groups, tiled=True)


def body(obstacles, particles, forces, neighbours, carried, factor, inverses):
    ring = [[RING * z + y for y in range(RING)] for z in range(DEPTH)]
    line = [[RING * z + y for z in range(DEPTH)] for y in range(RING)]
    sent = payload(forces, particles, neighbours).reshape(ROWS * COLS, SHARE, 128)
    got = lax.all_to_all(sent, ("row", "col"), 0, 0, tiled=True).reshape(ROWS * RHS, 128)
    rows = factor.transpose(0, 1, 3, 2, 4).reshape(2, COLUMNS * COMPS * BLOCKS_DEV, 128)
    fh, fl, lend, ih, il, mine, others = prepare(rows, inverses, carried)
    tiles = [lend]
    for step in range(1, RING):
        pairs = [(RING * z + (y + step) % RING, RING * z + y) for z in range(DEPTH) for y in range(RING)]
        tiles.append(lax.ppermute(lend, "row", pairs))
    near0, spread, push, places, flags = near_first(got, obstacles, mine)
    parts = lax.all_to_all(spread, "col", 0, 0, tiled=True)
    rest = near_rest(obstacles, push, places, flags)
    shares = along(first_solve(parts, ih, il, near0), ring)
    parts = along(add(shares), line)
    parts, rest = lax.optimization_barrier((parts, rest))
    first, spread = diagonal(parts, shares, tiles)
    parts = lax.all_to_all(spread, "col", 0, 0, tiled=True)
    parts = along(second_solve(parts, tiles), line)
    shares = along(gather(parts, first), ring)
    part, answers = change(shares, fh, fl, others, near0, rest)
    back = lax.all_to_all(part, "col", 0, 0, tiled=True)
    return (answers, jnp.sum(back, axis=0))


def solution(mesh):
    in_specs = (
        P(None, "row"),
        P(None, "row"),
        P(None, None, "row"),
        P("row", "col"),
        P("row", None, None, None),
        P(None, "col", "row", None, None),
        P(None, "row", "col"),
    )
    out_specs = (P(None, None, "col"), P("row", None, "col", None))
    return jax.shard_map(body, mesh=mesh, in_specs=in_specs, out_specs=out_specs, check_vma=False)
```

```python
import functools

import jax
import jax.numpy as jnp
from jax import lax
from jax.experimental import pallas as pl
from jax.experimental.pallas import tpu as pltpu
from jax.sharding import PartitionSpec as P

ROWS = 32
COLS = 8
BLOCKS_DEV = 4
SLICE = 32
RHS = 32
COMPS = 3
PAIRS = ((0, 0), (1, 1), (2, 2), (0, 1), (0, 2), (1, 2))
SHARE = RHS // COLS
COLUMNS = 512
RING = 4
DEPTH = 8
EIGHT = RHS // RING


ON_CHIP = pl.BlockSpec(memory_space=pltpu.VMEM)
IN_PLACE = pl.BlockSpec(memory_space=pltpu.HBM)
GRANT = pltpu.CompilerParams(vmem_limit_bytes=16 << 20)


def kept(shape, dtype=jnp.float32):
    return pltpu.VMEM(shape, dtype)


def keep(array):
    return pltpu.with_memory_space_constraint(array, pltpu.VMEM)


def stay(array):
    return pltpu.with_memory_space_constraint(array, pltpu.HBM)


def halves(value):
    high = value.astype(jnp.bfloat16)
    return high, (value - high.astype(jnp.float32)).astype(jnp.bfloat16)


def product(left, high, low):
    top, rest = halves(left)
    both = jnp.concatenate([top, rest], axis=0)
    full = jnp.dot(both, high, preferred_element_type=jnp.float32)
    part = jnp.dot(top, low, preferred_element_type=jnp.float32)
    count = left.shape[0]
    return full[:count] + full[count:] + part


def payload_kernel(
    forces_hbm, particles_hbm, neighbours_hbm, out_hbm, forces_ref, particles_ref, neighbours_ref, sent, read, wrote
):
    col = lax.axis_index("col")
    start = pl.multiple_of((col // 2) * 8, 8)
    copies = [
        pltpu.make_async_copy(forces_hbm.at[:, pl.ds(start, 8), :], forces_ref, read.at[0]),
        pltpu.make_async_copy(particles_hbm, particles_ref, read.at[1]),
        pltpu.make_async_copy(neighbours_hbm, neighbours_ref, read.at[2]),
    ]
    for copy in copies:
        copy.start()
    lane = lax.broadcasted_iota(jnp.int32, (8, 128), 1)
    line = lax.broadcasted_iota(jnp.int32, (8, 128), 0)
    odd = jnp.full((8, 128), col % 2, jnp.int32) == 1
    for copy in copies:
        copy.wait()
    for half in range(2):
        sides = []
        for comp in range(COMPS):
            eight = forces_ref[comp, :, pl.ds(128 * half, 128)]
            sides.append(jnp.where(odd, pltpu.roll(eight, 4, axis=0), eight))
        place = jnp.concatenate(
            [particles_ref[:, pl.ds(128 * half, 128)], jnp.zeros((5, 128), jnp.float32)], axis=0
        )
        listed = jnp.full((8, 128), -1.0, jnp.float32)
        for entry in range(4):
            name = jnp.full((8, 128), neighbours_ref[half, entry], jnp.int32).astype(jnp.float32)
            listed = jnp.where(lane == 96 + entry, name, listed)
        for quarter in range(4):
            value = None
            for at, piece in enumerate([*sides, place]):
                turn = (SLICE * (at - quarter)) % 128
                piece = pltpu.roll(piece, turn, axis=1) if turn else piece
                value = piece if value is None else jnp.where(lane >= SLICE * at, piece, value)
            value = jnp.where((lane >= 96) & (line == 3), listed, value)
            sent[4 * half + quarter] = value[0:4]
    copies = [pltpu.make_async_copy(sent, out_hbm.at[row], wrote.at[row]) for row in range(ROWS)]
    for copy in copies:
        copy.start()
    for copy in copies:
        copy.wait()


def payload(forces, particles, neighbours):
    return pl.pallas_call(
        payload_kernel,
        out_shape=pltpu.HBM((ROWS, COLS, SHARE, 128), jnp.float32),
        in_specs=[IN_PLACE] * 3,
        out_specs=IN_PLACE,
        scratch_shapes=[
            pltpu.VMEM((COMPS, 8, 256), jnp.float32),
            pltpu.VMEM((COMPS, 256), jnp.float32),
            pltpu.SMEM((2, 4), jnp.int32),
            pltpu.VMEM((COLS, SHARE, 128), jnp.float32),
            pltpu.SemaphoreType.DMA((3,)),
            pltpu.SemaphoreType.DMA((ROWS,)),
        ],
        name="payload",
        compiler_params=GRANT,
    )(stay(forces), stay(particles), stay(neighbours))


def prepare_kernel(
    factor_ref, inverses_ref, carried_ref, fh_ref, fl_ref, lend_ref, ih_ref, il_ref, mine_ref, others_ref
):
    for panel in range(2):
        for comp in range(COMPS):
            for block in range(BLOCKS_DEV):
                rows = pl.ds(BLOCKS_DEV * comp + block, COLUMNS, stride=COMPS * BLOCKS_DEV)
                value = factor_ref[panel, rows, :]
                high, low = halves(value)
                pair = 2 * comp + block // 2
                lanes = pl.ds(128 * (block % 2), 128)
                fh_ref[panel, pair, :, lanes] = high
                fl_ref[panel, pair, :, lanes] = low
                if panel == 0 and comp == 1 and block == 0:
                    for quarter in range(4):
                        lend_ref[quarter] = value[128 * quarter : 128 * quarter + 128]
    for quarter in range(4):
        lend_ref[4 + quarter] = inverses_ref[1, :, pl.ds(128 * quarter, 128)]
    high, low = halves(inverses_ref[0])
    ih_ref[...] = high
    il_ref[...] = low
    owner = lax.broadcasted_iota(jnp.int32, (RHS, 128), 0) // SHARE
    own = owner == jnp.full((RHS, 128), lax.axis_index("col"), jnp.int32)
    for block in range(BLOCKS_DEV):
        for comp in range(COMPS):
            value = jnp.where(own, carried_ref[block, comp], 0.0)
            if block == 0:
                mine_ref[comp] = value
            else:
                others_ref[block - 1, comp] = value


def prepare(factor_rows, inverses, carried):
    panels = (2, 2 * COMPS, COLUMNS, 256)
    return pl.pallas_call(
        prepare_kernel,
        out_shape=(
            pltpu.HBM(panels, jnp.bfloat16),
            pltpu.HBM(panels, jnp.bfloat16),
            kept((8, 128, 128)),
            kept((128, COLUMNS), jnp.bfloat16),
            kept((128, COLUMNS), jnp.bfloat16),
            kept((COMPS, RHS, 128)),
            pltpu.HBM((BLOCKS_DEV - 1, COMPS, RHS, 128), jnp.float32),
        ),
        in_specs=[ON_CHIP] * 3,
        out_specs=(ON_CHIP,) * 7,
        name="prepare",
        compiler_params=GRANT,
    )(factor_rows, inverses, carried)


def fill(places_ref, source):
    for comp in range(COMPS):
        for group in range(ROWS):
            column = places_ref[comp, :, group : group + 1]
            source[comp, pl.ds(SLICE * group, SLICE), :] = jnp.broadcast_to(column, (SLICE, 128))


def couple(blocks, points_ref, flags_ref, push_ref, source_ref, high, low):
    width = 128 * len(blocks)
    totals = [None] * COMPS
    for tile in range(4):
        slot = tile % 2
        for where, block in enumerate(blocks):
            lanes = pl.ds(128 * where, 128)
            points = [points_ref[c : c + 1, pl.ds(128 * block, 128)] for c in range(COMPS)]
            flags = flags_ref[block : block + 1, :]
            for at in range(8):
                group = 8 * tile + at
                rows = pl.ds(SLICE * at, SLICE)
                spots = pl.ds(SLICE * group, SLICE)
                diff = [points[c] - source_ref[c, spots, :] for c in range(COMPS)]
                flag = jnp.broadcast_to(flags[:, 8 * group : 8 * group + 1], (SLICE, 128))
                radius = diff[0] * diff[0] + diff[1] * diff[1] + diff[2] * diff[2] + 1.0
                root = lax.rsqrt(radius)
                cube = root * root * root * flag
                iso = (radius + 1.0) * cube
                scaled = [diff[0] * cube, diff[1] * cube, diff[2] * cube]
                for n, (a, b) in enumerate(PAIRS):
                    value = scaled[a] * diff[b]
                    top, rest = halves(value + iso if a == b else value)
                    high[slot, n, rows, lanes] = top
                    low[slot, n, rows, lanes] = rest
        for n, (a, b) in enumerate(PAIRS):
            if a == b:
                left, first = push_ref[b, tile], push_ref[b, tile, 0:32]
            else:
                left = jnp.concatenate([push_ref[b, tile], push_ref[a, tile]], axis=0)
                first = jnp.concatenate(
                    [push_ref[b, tile, 0:32], push_ref[a, tile, 0:32]], axis=0
                )
            full = jnp.dot(left, high[slot, n, :, 0:width], preferred_element_type=jnp.float32)
            rest = jnp.dot(first, low[slot, n, :, 0:width], preferred_element_type=jnp.float32)
            add = full[0:32] + full[32:64] + rest[0:32]
            totals[a] = add if totals[a] is None else totals[a] + add
            if a != b:
                add = full[64:96] + full[96:128] + rest[32:64]
                totals[b] = add if totals[b] is None else totals[b] + add
    return totals


def near_first_kernel(
    got_ref, points_ref, mine_ref, out_ref, spread_ref, push_ref, places_ref, flags_ref, source_ref, high, low
):
    lane = lax.broadcasted_iota(jnp.int32, (RHS, 128), 1) // SLICE
    for quad in range(8):
        for comp in range(COMPS):
            joined = None
            for at in range(4):
                piece = got_ref[pl.ds(RHS * (4 * quad + at), RHS), :]
                turn = (SLICE * (at - comp)) % 128
                piece = pltpu.roll(piece, turn, axis=1) if turn else piece
                joined = piece if joined is None else jnp.where(lane == at, piece, joined)
            top, rest = halves(joined)
            lanes = pl.ds(128 * (quad % 2), 128)
            push_ref[comp, quad // 2, 0:32, lanes] = top
            push_ref[comp, quad // 2, 32:64, lanes] = rest
    for comp in range(COMPS):
        places_ref[comp] = got_ref[pl.ds(comp, ROWS, stride=RHS), :].T[96:128, :]
    fill(places_ref, source_ref)
    lists = got_ref[pl.ds(3, ROWS * COLS, stride=4), :].T[96:104, :]
    first = BLOCKS_DEV * lax.axis_index("row")
    for block in range(BLOCKS_DEV):
        name = jnp.full(lists.shape, first + block, jnp.int32).astype(jnp.float32)
        found = jnp.where(lists == name, 1.0, 0.0)
        for step in (1, 2, 4):
            found = jnp.maximum(found, pltpu.roll(found, ROWS * COLS - step, axis=1))
        flags_ref[block : block + 1, :] = jnp.max(found, axis=0, keepdims=True)
    totals = couple((0,), points_ref, flags_ref, push_ref, source_ref, high, low)
    for comp in range(COMPS):
        value = totals[comp] + mine_ref[comp]
        out_ref[comp] = value
        if comp == 0:
            for part in range(COLS):
                spread_ref[part] = value


def near_first(got, points, mine):
    return pl.pallas_call(
        near_first_kernel,
        out_shape=(
            kept((COMPS, RHS, 128)),
            kept((COLS, RHS, 128)),
            kept((COMPS, 4, 64, 256), jnp.bfloat16),
            kept((COMPS, SLICE, ROWS)),
            kept((BLOCKS_DEV, 256)),
        ),
        in_specs=[ON_CHIP] * 3,
        out_specs=(ON_CHIP,) * 5,
        scratch_shapes=[pltpu.VMEM((COMPS, ROWS * SLICE, 128), jnp.float32)]
        + [pltpu.VMEM((2, 6, 256, 128), jnp.bfloat16)] * 2,
        name="near_first",
        compiler_params=GRANT,
    )(keep(got), points, keep(mine))


def near_rest_kernel(
    points_ref, push_ref, places_ref, flags_ref, out_ref, source_ref, high, low
):
    fill(places_ref, source_ref)
    for blocks in ((1, 2), (3,)):
        totals = couple(blocks, points_ref, flags_ref, push_ref, source_ref, high, low)
        for where, block in enumerate(blocks):
            for comp in range(COMPS):
                out_ref[block - 1, comp] = totals[comp][:, 128 * where : 128 * where + 128]


def near_rest(points, push, places, flags):
    return pl.pallas_call(
        near_rest_kernel,
        out_shape=kept((BLOCKS_DEV - 1, COMPS, RHS, 128)),
        in_specs=[ON_CHIP] * 4,
        out_specs=ON_CHIP,
        scratch_shapes=[pltpu.VMEM((COMPS, ROWS * SLICE, 128), jnp.float32)]
        + [pltpu.VMEM((2, 6, 256, 256), jnp.bfloat16)] * 2,
        name="near_rest",
        compiler_params=GRANT,
    )(points, keep(push), keep(places), keep(flags))


def total(parts_ref):
    value = parts_ref[0]
    for part in range(1, parts_ref.shape[0]):
        value = value + parts_ref[part]
    return value


def first_solve_kernel(parts_ref, ih_ref, il_ref, near_ref, out_ref):
    value = product(total(parts_ref), ih_ref[...], il_ref[...])
    for y in range(RING):
        sides = slice(EIGHT * y, EIGHT * y + EIGHT)
        for quarter in range(4):
            out_ref[y, pl.ds(EIGHT * quarter, EIGHT), :] = value[sides, 128 * quarter : 128 * quarter + 128]
        out_ref[y, pl.ds(32, EIGHT), :] = near_ref[1, pl.ds(EIGHT * y, EIGHT), :]


def first_solve(parts, ih, il, near):
    return pl.pallas_call(
        first_solve_kernel,
        out_shape=kept((RING, 40, 128)),
        in_specs=[ON_CHIP] * 4,
        out_specs=ON_CHIP,
        name="first_solve",
        compiler_params=GRANT,
    )(keep(parts), keep(ih), keep(il), keep(near))


def add_kernel(got_ref, out_ref):
    value = total(got_ref)[0:32]
    for part in range(DEPTH):
        out_ref[part] = value


def add(got):
    return pl.pallas_call(
        add_kernel,
        out_shape=kept((DEPTH, 32, 128)),
        in_specs=[ON_CHIP],
        out_specs=ON_CHIP,
        name="add",
        compiler_params=GRANT,
    )(keep(got))


def wide(value):
    return jnp.concatenate([value[EIGHT * q : EIGHT * q + EIGHT] for q in range(4)], axis=1)


def diagonal_kernel(parts_ref, got_ref, own_ref, one_ref, two_ref, three_ref, answer_ref, out_ref):
    value = total(parts_ref)
    answer_ref[...] = value
    answer = wide(value)
    y = lax.axis_index("row") % RING
    for step, tiles in enumerate((own_ref, one_ref, two_ref, three_ref)):
        columns = jnp.concatenate([tiles[quarter] for quarter in range(4)], axis=0)
        base = got_ref[(y + step) % RING, pl.ds(32, EIGHT), :]
        value = base - product(answer, *halves(columns))
        for part in range(COLS):
            out_ref[part, pl.ds(EIGHT * step, EIGHT), :] = value


def diagonal(parts, got, tiles):
    return pl.pallas_call(
        diagonal_kernel,
        out_shape=(kept((32, 128)), kept((COLS, 32, 128))),
        in_specs=[ON_CHIP] * 6,
        out_specs=(ON_CHIP,) * 2,
        name="diagonal",
        compiler_params=GRANT,
    )(keep(parts), keep(got), *[keep(tile) for tile in tiles])


def second_solve_kernel(parts_ref, own_ref, one_ref, two_ref, three_ref, out_ref):
    diag = total(parts_ref)
    value = None
    for step, tiles in enumerate((own_ref, one_ref, two_ref, three_ref)):
        inverse = jnp.concatenate([tiles[4 + quarter] for quarter in range(4)], axis=1)
        add = product(diag[EIGHT * step : EIGHT * step + EIGHT], *halves(inverse))
        value = add if value is None else value + add
    for part in range(DEPTH):
        for quarter in range(4):
            out_ref[part, pl.ds(EIGHT * quarter, EIGHT), :] = value[:, 128 * quarter : 128 * quarter + 128]


def second_solve(parts, tiles):
    return pl.pallas_call(
        second_solve_kernel,
        out_shape=kept((DEPTH, 32, 128)),
        in_specs=[ON_CHIP] * 5,
        out_specs=ON_CHIP,
        name="second_solve",
        compiler_params=GRANT,
    )(keep(parts), *[keep(tile) for tile in tiles])


def gather_kernel(parts_ref, first_ref, out_ref):
    second = total(parts_ref)
    for y in range(RING):
        out_ref[y, 0:32] = first_ref[...]
        out_ref[y, 32:64] = second


def gather(parts, first):
    return pl.pallas_call(
        gather_kernel,
        out_shape=kept((RING, 64, 128)),
        in_specs=[ON_CHIP] * 2,
        out_specs=ON_CHIP,
        name="gather",
        compiler_params=GRANT,
    )(keep(parts), keep(first))


def whole(got_ref, panel):
    columns = []
    for quarter in range(4):
        rows = pl.ds(32 * panel + EIGHT * quarter, EIGHT)
        columns.append(jnp.concatenate([got_ref[y, rows, :] for y in range(RING)], axis=0))
    return jnp.concatenate(columns, axis=1)


def change_kernel(
    got_ref, fh_hbm, fl_hbm, others_hbm, first_ref, rest_ref, out_ref, answers_hbm,
    high, low, others, both, read, extra
):
    jobs, copies = [], []
    for comp in range(COMPS):
        for pair in range(2):
            for panel in range(2):
                at = len(jobs)
                hidden = pair == 0 and comp <= panel
                lanes = pl.ds(128, 128) if hidden else pl.ds(0, 256)
                jobs.append((comp, pair, panel, hidden, lanes))
                for side, (source, target) in enumerate(((fh_hbm, high), (fl_hbm, low))):
                    copies.append(
                        pltpu.make_async_copy(
                            source.at[panel, 2 * comp + pair, :, lanes],
                            target.at[at, :, lanes],
                            read.at[2 * at + side],
                        )
                    )
    carry = pltpu.make_async_copy(others_hbm, others, extra.at[0])
    carry.start()
    ahead = 24
    for copy in copies[:ahead]:
        copy.start()
    sides = [whole(got_ref, panel) for panel in range(2)]
    both[0], both[1] = sides
    answer = pltpu.make_async_copy(both, answers_hbm, extra.at[1])
    answer.start()
    carry.wait()
    group = 6
    for first in range(0, len(jobs), group):
        for copy in copies[2 * first : 2 * (first + group)]:
            copy.wait()
        for copy in copies[2 * first + ahead : 2 * (first + group) + ahead]:
            copy.start()
        moved = {}
        for at in range(first, first + group):
            comp, pair, panel, hidden, lanes = jobs[at]
            moved[comp, pair, panel] = product(sides[panel], high[at, :, lanes], low[at, :, lanes])
        for comp, pair, panel in list(moved):
            if panel == 0:
                continue
            for where in range(2):
                block = 2 * pair + where
                if block == 0:
                    value = first_ref[comp]
                else:
                    value = rest_ref[block - 1, comp] + others[block - 1, comp]
                for index in range(2):
                    part = moved[comp, pair, index]
                    if block > 0 or comp > index:
                        start = part.shape[1] - 256 + 128 * where
                        value = value - part[:, start : start + 128]
                for part in range(COLS):
                    out_ref[part, block, comp] = value[SHARE * part : SHARE * part + SHARE]
    answer.wait()


def change(got, fh, fl, others, first, rest):
    return pl.pallas_call(
        change_kernel,
        out_shape=(
            kept((COLS, BLOCKS_DEV, COMPS, SHARE, 128)),
            pltpu.HBM((2, RHS, COLUMNS), jnp.float32),
        ),
        in_specs=[ON_CHIP, IN_PLACE, IN_PLACE, IN_PLACE, ON_CHIP, ON_CHIP],
        out_specs=(ON_CHIP, IN_PLACE),
        scratch_shapes=[
            pltpu.VMEM((4 * COMPS, COLUMNS, 256), jnp.bfloat16),
            pltpu.VMEM((4 * COMPS, COLUMNS, 256), jnp.bfloat16),
            pltpu.VMEM((BLOCKS_DEV - 1, COMPS, RHS, 128), jnp.float32),
            pltpu.VMEM((2, RHS, COLUMNS), jnp.float32),
            pltpu.SemaphoreType.DMA((8 * COMPS,)),
            pltpu.SemaphoreType.DMA((2,)),
        ],
        name="change",
        compiler_params=GRANT,
    )(keep(got), stay(fh), stay(fl), stay(others), keep(first), keep(rest))


def along(array, groups):
    return lax.all_to_all(array, "row", 0, 0, axis_index_groups=groups, tiled=True)


def body(obstacles, particles, forces, neighbours, carried, factor, inverses):
    ring = [[RING * z + y for y in range(RING)] for z in range(DEPTH)]
    line = [[RING * z + y for z in range(DEPTH)] for y in range(RING)]
    sent = payload(forces, particles, neighbours).reshape(ROWS * COLS, SHARE, 128)
    got = lax.all_to_all(sent, ("row", "col"), 0, 0, tiled=True).reshape(ROWS * RHS, 128)
    rows = factor.transpose(0, 1, 3, 2, 4).reshape(2, COLUMNS * COMPS * BLOCKS_DEV, 128)
    fh, fl, lend, ih, il, mine, others = prepare(rows, inverses, carried)
    tiles = [lend]
    for step in range(1, RING):
        pairs = [(RING * z + (y + step) % RING, RING * z + y) for z in range(DEPTH) for y in range(RING)]
        tiles.append(lax.ppermute(lend, "row", pairs))
    near0, spread, push, places, flags = near_first(got, obstacles, mine)
    parts = lax.all_to_all(spread, "col", 0, 0, tiled=True)
    rest = near_rest(obstacles, push, places, flags)
    shares = along(first_solve(parts, ih, il, near0), ring)
    parts = along(add(shares), line)
    parts, rest = lax.optimization_barrier((parts, rest))
    first, spread = diagonal(parts, shares, tiles)
    parts = lax.all_to_all(spread, "col", 0, 0, tiled=True)
    parts = along(second_solve(parts, tiles), line)
    shares = along(gather(parts, first), ring)
    part, answers = change(shares, fh, fl, others, near0, rest)
    back = lax.all_to_all(part, "col", 0, 0, tiled=True)
    return (answers, jnp.sum(back, axis=0))


def solution(mesh):
    in_specs = (
        P(None, "row"),
        P(None, "row"),
        P(None, None, "row"),
        P("row", "col"),
        P("row", None, None, None),
        P(None, "col", "row", None, None),
        P(None, "row", "col"),
    )
    out_specs = (P(None, None, "col"), P("row", None, "col", None))
    return jax.shard_map(body, mesh=mesh, in_specs=in_specs, out_specs=out_specs, check_vma=False)
```

```python
import functools

import jax
import jax.numpy as jnp
from jax import lax
from jax.experimental import pallas as pl
from jax.experimental.pallas import tpu as pltpu
from jax.sharding import PartitionSpec as P

ROWS = 32
COLS = 8
BLOCKS_DEV = 4
SLICE = 32
RHS = 32
COMPS = 3
PAIRS = ((0, 0), (1, 1), (2, 2), (0, 1), (0, 2), (1, 2))
SHARE = RHS // COLS
COLUMNS = 512
RING = 4
DEPTH = 8
EIGHT = RHS // RING


ON_CHIP = pl.BlockSpec(memory_space=pltpu.VMEM)
IN_PLACE = pl.BlockSpec(memory_space=pltpu.HBM)
GRANT = pltpu.CompilerParams(vmem_limit_bytes=16 << 20)


def kept(shape, dtype=jnp.float32):
    return pltpu.VMEM(shape, dtype)


def keep(array):
    return pltpu.with_memory_space_constraint(array, pltpu.VMEM)


def stay(array):
    return pltpu.with_memory_space_constraint(array, pltpu.HBM)


def halves(value):
    high = value.astype(jnp.bfloat16)
    return high, (value - high.astype(jnp.float32)).astype(jnp.bfloat16)


def product(left, high, low):
    top, rest = halves(left)
    both = jnp.concatenate([top, rest], axis=0)
    full = jnp.dot(both, high, preferred_element_type=jnp.float32)
    part = jnp.dot(top, low, preferred_element_type=jnp.float32)
    count = left.shape[0]
    return full[:count] + full[count:] + part


def payload_kernel(
    forces_hbm, particles_hbm, neighbours_hbm, out_hbm, forces_ref, particles_ref, neighbours_ref, sent, read, wrote
):
    col = lax.axis_index("col")
    start = pl.multiple_of((col // 2) * 8, 8)
    copies = [
        pltpu.make_async_copy(forces_hbm.at[:, pl.ds(start, 8), :], forces_ref, read.at[0]),
        pltpu.make_async_copy(particles_hbm, particles_ref, read.at[1]),
        pltpu.make_async_copy(neighbours_hbm, neighbours_ref, read.at[2]),
    ]
    for copy in copies:
        copy.start()
    lane = lax.broadcasted_iota(jnp.int32, (8, 128), 1)
    line = lax.broadcasted_iota(jnp.int32, (8, 128), 0)
    odd = jnp.full((8, 128), col % 2, jnp.int32) == 1
    for copy in copies:
        copy.wait()
    for half in range(2):
        sides = []
        for comp in range(COMPS):
            eight = forces_ref[comp, :, pl.ds(128 * half, 128)]
            sides.append(jnp.where(odd, pltpu.roll(eight, 4, axis=0), eight))
        place = jnp.concatenate(
            [particles_ref[:, pl.ds(128 * half, 128)], jnp.zeros((5, 128), jnp.float32)], axis=0
        )
        listed = jnp.full((8, 128), -1.0, jnp.float32)
        for entry in range(4):
            name = jnp.full((8, 128), neighbours_ref[half, entry], jnp.int32).astype(jnp.float32)
            listed = jnp.where(lane == 96 + entry, name, listed)
        for quarter in range(4):
            value = None
            for at, piece in enumerate([*sides, place]):
                turn = (SLICE * (at - quarter)) % 128
                piece = pltpu.roll(piece, turn, axis=1) if turn else piece
                value = piece if value is None else jnp.where(lane >= SLICE * at, piece, value)
            value = jnp.where((lane >= 96) & (line == 3), listed, value)
            sent[4 * half + quarter] = value[0:4]
    copies = [pltpu.make_async_copy(sent, out_hbm.at[row], wrote.at[row]) for row in range(ROWS)]
    for copy in copies:
        copy.start()
    for copy in copies:
        copy.wait()


def payload(forces, particles, neighbours):
    return pl.pallas_call(
        payload_kernel,
        out_shape=pltpu.HBM((ROWS, COLS, SHARE, 128), jnp.float32),
        in_specs=[IN_PLACE] * 3,
        out_specs=IN_PLACE,
        scratch_shapes=[
            pltpu.VMEM((COMPS, 8, 256), jnp.float32),
            pltpu.VMEM((COMPS, 256), jnp.float32),
            pltpu.SMEM((2, 4), jnp.int32),
            pltpu.VMEM((COLS, SHARE, 128), jnp.float32),
            pltpu.SemaphoreType.DMA((3,)),
            pltpu.SemaphoreType.DMA((ROWS,)),
        ],
        name="payload",
        compiler_params=GRANT,
    )(stay(forces), stay(particles), stay(neighbours))


def prepare_kernel(
    factor_ref, inverses_ref, carried_ref, fh_ref, fl_ref, lend_ref, ih_ref, il_ref, mine_ref, others_ref
):
    for panel in range(2):
        for comp in range(COMPS):
            for block in range(BLOCKS_DEV):
                rows = pl.ds(BLOCKS_DEV * comp + block, COLUMNS, stride=COMPS * BLOCKS_DEV)
                value = factor_ref[panel, rows, :]
                high, low = halves(value)
                pair = 2 * comp + block // 2
                lanes = pl.ds(128 * (block % 2), 128)
                fh_ref[panel, pair, :, lanes] = high
                fl_ref[panel, pair, :, lanes] = low
                if panel == 0 and comp == 1 and block == 0:
                    for quarter in range(4):
                        lend_ref[quarter] = value[128 * quarter : 128 * quarter + 128]
    for quarter in range(4):
        lend_ref[4 + quarter] = inverses_ref[1, :, pl.ds(128 * quarter, 128)]
    high, low = halves(inverses_ref[0])
    ih_ref[...] = high
    il_ref[...] = low
    owner = lax.broadcasted_iota(jnp.int32, (RHS, 128), 0) // SHARE
    own = owner == jnp.full((RHS, 128), lax.axis_index("col"), jnp.int32)
    for block in range(BLOCKS_DEV):
        for comp in range(COMPS):
            value = jnp.where(own, carried_ref[block, comp], 0.0)
            if block == 0:
                mine_ref[comp] = value
            else:
                others_ref[block - 1, comp] = value


def prepare(factor_rows, inverses, carried):
    panels = (2, 2 * COMPS, COLUMNS, 256)
    return pl.pallas_call(
        prepare_kernel,
        out_shape=(
            pltpu.HBM(panels, jnp.bfloat16),
            pltpu.HBM(panels, jnp.bfloat16),
            kept((8, 128, 128)),
            kept((128, COLUMNS), jnp.bfloat16),
            kept((128, COLUMNS), jnp.bfloat16),
            kept((COMPS, RHS, 128)),
            pltpu.HBM((BLOCKS_DEV - 1, COMPS, RHS, 128), jnp.float32),
        ),
        in_specs=[ON_CHIP] * 3,
        out_specs=(ON_CHIP,) * 7,
        name="prepare",
        compiler_params=GRANT,
    )(factor_rows, inverses, carried)


def fill(places_ref, source):
    for comp in range(COMPS):
        for group in range(ROWS):
            column = places_ref[comp, :, group : group + 1]
            source[comp, pl.ds(SLICE * group, SLICE), :] = jnp.broadcast_to(column, (SLICE, 128))


def couple(blocks, points_ref, flags_ref, push_ref, source_ref, high, low):
    width = 128 * len(blocks)
    totals = [None] * COMPS
    for tile in range(4):
        slot = tile % 2
        for where, block in enumerate(blocks):
            lanes = pl.ds(128 * where, 128)
            points = [points_ref[c : c + 1, pl.ds(128 * block, 128)] for c in range(COMPS)]
            flags = flags_ref[block : block + 1, :]
            for at in range(8):
                group = 8 * tile + at
                rows = pl.ds(SLICE * at, SLICE)
                spots = pl.ds(SLICE * group, SLICE)
                diff = [points[c] - source_ref[c, spots, :] for c in range(COMPS)]
                flag = jnp.broadcast_to(flags[:, 8 * group : 8 * group + 1], (SLICE, 128))
                radius = diff[0] * diff[0] + diff[1] * diff[1] + diff[2] * diff[2] + 1.0
                root = lax.rsqrt(radius)
                cube = root * root * root * flag
                iso = (radius + 1.0) * cube
                scaled = [diff[0] * cube, diff[1] * cube, diff[2] * cube]
                for n, (a, b) in enumerate(PAIRS):
                    value = scaled[a] * diff[b]
                    top, rest = halves(value + iso if a == b else value)
                    high[slot, n, rows, lanes] = top
                    low[slot, n, rows, lanes] = rest
        for n, (a, b) in enumerate(PAIRS):
            if a == b:
                left, first = push_ref[b, tile], push_ref[b, tile, 0:32]
            else:
                left = jnp.concatenate([push_ref[b, tile], push_ref[a, tile]], axis=0)
                first = jnp.concatenate(
                    [push_ref[b, tile, 0:32], push_ref[a, tile, 0:32]], axis=0
                )
            full = jnp.dot(left, high[slot, n, :, 0:width], preferred_element_type=jnp.float32)
            rest = jnp.dot(first, low[slot, n, :, 0:width], preferred_element_type=jnp.float32)
            add = full[0:32] + full[32:64] + rest[0:32]
            totals[a] = add if totals[a] is None else totals[a] + add
            if a != b:
                add = full[64:96] + full[96:128] + rest[32:64]
                totals[b] = add if totals[b] is None else totals[b] + add
    return totals


def near_first_kernel(
    got_ref, points_ref, mine_ref, out_ref, spread_ref, push_ref, places_ref, flags_ref, source_ref, high, low
):
    lane = lax.broadcasted_iota(jnp.int32, (RHS, 128), 1) // SLICE
    for quad in range(8):
        for comp in range(COMPS):
            joined = None
            for at in range(4):
                piece = got_ref[pl.ds(RHS * (4 * quad + at), RHS), :]
                turn = (SLICE * (at - comp)) % 128
                piece = pltpu.roll(piece, turn, axis=1) if turn else piece
                joined = piece if joined is None else jnp.where(lane == at, piece, joined)
            top, rest = halves(joined)
            lanes = pl.ds(128 * (quad % 2), 128)
            push_ref[comp, quad // 2, 0:32, lanes] = top
            push_ref[comp, quad // 2, 32:64, lanes] = rest
    for comp in range(COMPS):
        places_ref[comp] = got_ref[pl.ds(comp, ROWS, stride=RHS), :].T[96:128, :]
    fill(places_ref, source_ref)
    lists = got_ref[pl.ds(3, ROWS * COLS, stride=4), :].T[96:104, :]
    first = BLOCKS_DEV * lax.axis_index("row")
    for block in range(BLOCKS_DEV):
        name = jnp.full(lists.shape, first + block, jnp.int32).astype(jnp.float32)
        found = jnp.where(lists == name, 1.0, 0.0)
        for step in (1, 2, 4):
            found = jnp.maximum(found, pltpu.roll(found, ROWS * COLS - step, axis=1))
        flags_ref[block : block + 1, :] = jnp.max(found, axis=0, keepdims=True)
    totals = couple((0,), points_ref, flags_ref, push_ref, source_ref, high, low)
    for comp in range(COMPS):
        value = totals[comp] + mine_ref[comp]
        out_ref[comp] = value
        if comp == 0:
            for part in range(COLS):
                spread_ref[part] = value


def near_first(got, points, mine):
    return pl.pallas_call(
        near_first_kernel,
        out_shape=(
            kept((COMPS, RHS, 128)),
            kept((COLS, RHS, 128)),
            kept((COMPS, 4, 64, 256), jnp.bfloat16),
            kept((COMPS, SLICE, ROWS)),
            kept((BLOCKS_DEV, 256)),
        ),
        in_specs=[ON_CHIP] * 3,
        out_specs=(ON_CHIP,) * 5,
        scratch_shapes=[pltpu.VMEM((COMPS, ROWS * SLICE, 128), jnp.float32)]
        + [pltpu.VMEM((2, 6, 256, 128), jnp.bfloat16)] * 2,
        name="near_first",
        compiler_params=GRANT,
    )(keep(got), points, keep(mine))


def near_rest_kernel(
    points_ref, push_ref, places_ref, flags_ref, out_ref, source_ref, high, low
):
    fill(places_ref, source_ref)
    for blocks in ((1, 2), (3,)):
        totals = couple(blocks, points_ref, flags_ref, push_ref, source_ref, high, low)
        for where, block in enumerate(blocks):
            for comp in range(COMPS):
                out_ref[block - 1, comp] = totals[comp][:, 128 * where : 128 * where + 128]


def near_rest(points, push, places, flags):
    return pl.pallas_call(
        near_rest_kernel,
        out_shape=kept((BLOCKS_DEV - 1, COMPS, RHS, 128)),
        in_specs=[ON_CHIP] * 4,
        out_specs=ON_CHIP,
        scratch_shapes=[pltpu.VMEM((COMPS, ROWS * SLICE, 128), jnp.float32)]
        + [pltpu.VMEM((2, 6, 256, 256), jnp.bfloat16)] * 2,
        name="near_rest",
        compiler_params=GRANT,
    )(points, keep(push), keep(places), keep(flags))


def total(parts_ref):
    value = parts_ref[0]
    for part in range(1, parts_ref.shape[0]):
        value = value + parts_ref[part]
    return value


def first_solve_kernel(parts_ref, ih_ref, il_ref, near_ref, out_ref):
    value = product(total(parts_ref), ih_ref[...], il_ref[...])
    for y in range(RING):
        sides = slice(EIGHT * y, EIGHT * y + EIGHT)
        for quarter in range(4):
            out_ref[y, pl.ds(EIGHT * quarter, EIGHT), :] = value[sides, 128 * quarter : 128 * quarter + 128]
        out_ref[y, pl.ds(32, EIGHT), :] = near_ref[1, pl.ds(EIGHT * y, EIGHT), :]


def first_solve(parts, ih, il, near):
    return pl.pallas_call(
        first_solve_kernel,
        out_shape=kept((RING, 40, 128)),
        in_specs=[ON_CHIP] * 4,
        out_specs=ON_CHIP,
        name="first_solve",
        compiler_params=GRANT,
    )(keep(parts), keep(ih), keep(il), keep(near))


def add_kernel(got_ref, out_ref):
    value = total(got_ref)[0:32]
    for part in range(DEPTH):
        out_ref[part] = value


def add(got):
    return pl.pallas_call(
        add_kernel,
        out_shape=kept((DEPTH, 32, 128)),
        in_specs=[ON_CHIP],
        out_specs=ON_CHIP,
        name="add",
        compiler_params=GRANT,
    )(keep(got))


def wide(value):
    return jnp.concatenate([value[EIGHT * q : EIGHT * q + EIGHT] for q in range(4)], axis=1)


def diagonal_kernel(parts_ref, got_ref, own_ref, one_ref, two_ref, three_ref, answer_ref, out_ref):
    value = total(parts_ref)
    answer_ref[...] = value
    answer = wide(value)
    y = lax.axis_index("row") % RING
    for step, tiles in enumerate((own_ref, one_ref, two_ref, three_ref)):
        columns = jnp.concatenate([tiles[quarter] for quarter in range(4)], axis=0)
        base = got_ref[(y + step) % RING, pl.ds(32, EIGHT), :]
        value = base - product(answer, *halves(columns))
        for part in range(COLS):
            out_ref[part, pl.ds(EIGHT * step, EIGHT), :] = value


def diagonal(parts, got, tiles):
    return pl.pallas_call(
        diagonal_kernel,
        out_shape=(kept((32, 128)), kept((COLS, 32, 128))),
        in_specs=[ON_CHIP] * 6,
        out_specs=(ON_CHIP,) * 2,
        name="diagonal",
        compiler_params=GRANT,
    )(keep(parts), keep(got), *[keep(tile) for tile in tiles])


def second_solve_kernel(parts_ref, own_ref, one_ref, two_ref, three_ref, out_ref):
    diag = total(parts_ref)
    value = None
    for step, tiles in enumerate((own_ref, one_ref, two_ref, three_ref)):
        inverse = jnp.concatenate([tiles[4 + quarter] for quarter in range(4)], axis=1)
        add = product(diag[EIGHT * step : EIGHT * step + EIGHT], *halves(inverse))
        value = add if value is None else value + add
    for part in range(DEPTH):
        for quarter in range(4):
            out_ref[part, pl.ds(EIGHT * quarter, EIGHT), :] = value[:, 128 * quarter : 128 * quarter + 128]


def second_solve(parts, tiles):
    return pl.pallas_call(
        second_solve_kernel,
        out_shape=kept((DEPTH, 32, 128)),
        in_specs=[ON_CHIP] * 5,
        out_specs=ON_CHIP,
        name="second_solve",
        compiler_params=GRANT,
    )(keep(parts), *[keep(tile) for tile in tiles])


def gather_kernel(parts_ref, first_ref, out_ref):
    second = total(parts_ref)
    for y in range(RING):
        out_ref[y, 0:32] = first_ref[...]
        out_ref[y, 32:64] = second


def gather(parts, first):
    return pl.pallas_call(
        gather_kernel,
        out_shape=kept((RING, 64, 128)),
        in_specs=[ON_CHIP] * 2,
        out_specs=ON_CHIP,
        name="gather",
        compiler_params=GRANT,
    )(keep(parts), keep(first))


def whole(got_ref, panel):
    columns = []
    for quarter in range(4):
        rows = pl.ds(32 * panel + EIGHT * quarter, EIGHT)
        columns.append(jnp.concatenate([got_ref[y, rows, :] for y in range(RING)], axis=0))
    return jnp.concatenate(columns, axis=1)


def change_kernel(
    got_ref, fh_hbm, fl_hbm, others_hbm, first_ref, rest_ref, out_ref, answers_hbm,
    high, low, others, both, read, extra
):
    jobs, copies = [], []
    for comp in range(COMPS):
        for pair in range(2):
            for panel in range(2):
                at = len(jobs)
                hidden = pair == 0 and comp <= panel
                lanes = pl.ds(128, 128) if hidden else pl.ds(0, 256)
                jobs.append((comp, pair, panel, hidden, lanes))
                for side, (source, target) in enumerate(((fh_hbm, high), (fl_hbm, low))):
                    copies.append(
                        pltpu.make_async_copy(
                            source.at[panel, 2 * comp + pair, :, lanes],
                            target.at[at, :, lanes],
                            read.at[2 * at + side],
                        )
                    )
    carry = pltpu.make_async_copy(others_hbm, others, extra.at[0])
    carry.start()
    ahead = 24
    for copy in copies[:ahead]:
        copy.start()
    sides = [whole(got_ref, panel) for panel in range(2)]
    both[0], both[1] = sides
    answer = pltpu.make_async_copy(both, answers_hbm, extra.at[1])
    answer.start()
    carry.wait()
    group = 6
    for first in range(0, len(jobs), group):
        for copy in copies[2 * first : 2 * (first + group)]:
            copy.wait()
        for copy in copies[2 * first + ahead : 2 * (first + group) + ahead]:
            copy.start()
        moved = {}
        for at in range(first, first + group):
            comp, pair, panel, hidden, lanes = jobs[at]
            moved[comp, pair, panel] = product(sides[panel], high[at, :, lanes], low[at, :, lanes])
        for comp, pair, panel in list(moved):
            if panel == 0:
                continue
            for where in range(2):
                block = 2 * pair + where
                if block == 0:
                    value = first_ref[comp]
                else:
                    value = rest_ref[block - 1, comp] + others[block - 1, comp]
                for index in range(2):
                    part = moved[comp, pair, index]
                    if block > 0 or comp > index:
                        start = part.shape[1] - 256 + 128 * where
                        value = value - part[:, start : start + 128]
                for part in range(COLS):
                    out_ref[part, block, comp] = value[SHARE * part : SHARE * part + SHARE]
    answer.wait()


def change(got, fh, fl, others, first, rest):
    return pl.pallas_call(
        change_kernel,
        out_shape=(
            kept((COLS, BLOCKS_DEV, COMPS, SHARE, 128)),
            pltpu.HBM((2, RHS, COLUMNS), jnp.float32),
        ),
        in_specs=[ON_CHIP, IN_PLACE, IN_PLACE, IN_PLACE, ON_CHIP, ON_CHIP],
        out_specs=(ON_CHIP, IN_PLACE),
        scratch_shapes=[
            pltpu.VMEM((4 * COMPS, COLUMNS, 256), jnp.bfloat16),
            pltpu.VMEM((4 * COMPS, COLUMNS, 256), jnp.bfloat16),
            pltpu.VMEM((BLOCKS_DEV - 1, COMPS, RHS, 128), jnp.float32),
            pltpu.VMEM((2, RHS, COLUMNS), jnp.float32),
            pltpu.SemaphoreType.DMA((8 * COMPS,)),
            pltpu.SemaphoreType.DMA((2,)),
        ],
        name="change",
        compiler_params=GRANT,
    )(keep(got), stay(fh), stay(fl), stay(others), keep(first), keep(rest))


def along(array, groups):
    return lax.all_to_all(array, "row", 0, 0, axis_index_groups=groups, tiled=True)


def body(obstacles, particles, forces, neighbours, carried, factor, inverses):
    ring = [[RING * z + y for y in range(RING)] for z in range(DEPTH)]
    line = [[RING * z + y for z in range(DEPTH)] for y in range(RING)]
    sent = payload(forces, particles, neighbours).reshape(ROWS * COLS, SHARE, 128)
    got = lax.all_to_all(sent, ("row", "col"), 0, 0, tiled=True).reshape(ROWS * RHS, 128)
    rows = factor.transpose(0, 1, 3, 2, 4).reshape(2, COLUMNS * COMPS * BLOCKS_DEV, 128)
    fh, fl, lend, ih, il, mine, others = prepare(rows, inverses, carried)
    tiles = [lend]
    for step in range(1, RING):
        pairs = [(RING * z + (y + step) % RING, RING * z + y) for z in range(DEPTH) for y in range(RING)]
        tiles.append(lax.ppermute(lend, "row", pairs))
    near0, spread, push, places, flags = near_first(got, obstacles, mine)
    parts = lax.all_to_all(spread, "col", 0, 0, tiled=True)
    rest = near_rest(obstacles, push, places, flags)
    shares = along(first_solve(parts, ih, il, near0), ring)
    shares, rest, *tiles = lax.optimization_barrier((shares, rest, *tiles))
    parts = along(add(shares), line)
    first, spread = diagonal(parts, shares, tiles)
    parts = lax.all_to_all(spread, "col", 0, 0, tiled=True)
    parts = along(second_solve(parts, tiles), line)
    shares = along(gather(parts, first), ring)
    part, answers = change(shares, fh, fl, others, near0, rest)
    back = lax.all_to_all(part, "col", 0, 0, tiled=True)
    return (answers, jnp.sum(back, axis=0))


def solution(mesh):
    in_specs = (
        P(None, "row"),
        P(None, "row"),
        P(None, None, "row"),
        P("row", "col"),
        P("row", None, None, None),
        P(None, "col", "row", None, None),
        P(None, "row", "col"),
    )
    out_specs = (P(None, None, "col"), P("row", None, "col", None))
    return jax.shard_map(body, mesh=mesh, in_specs=in_specs, out_specs=out_specs, check_vma=False)
```

```python
import functools

import jax
import jax.numpy as jnp
from jax import lax
from jax.experimental import pallas as pl
from jax.experimental.pallas import tpu as pltpu
from jax.sharding import PartitionSpec as P

ROWS = 32
COLS = 8
BLOCKS_DEV = 4
SLICE = 32
RHS = 32
COMPS = 3
PAIRS = ((0, 0), (1, 1), (2, 2), (0, 1), (0, 2), (1, 2))
SHARE = RHS // COLS
COLUMNS = 512
RING = 4
DEPTH = 8
EIGHT = RHS // RING


ON_CHIP = pl.BlockSpec(memory_space=pltpu.VMEM)
IN_PLACE = pl.BlockSpec(memory_space=pltpu.HBM)
GRANT = pltpu.CompilerParams(vmem_limit_bytes=16 << 20)


def kept(shape, dtype=jnp.float32):
    return pltpu.VMEM(shape, dtype)


def keep(array):
    return pltpu.with_memory_space_constraint(array, pltpu.VMEM)


def stay(array):
    return pltpu.with_memory_space_constraint(array, pltpu.HBM)


def halves(value):
    high = value.astype(jnp.bfloat16)
    return high, (value - high.astype(jnp.float32)).astype(jnp.bfloat16)


def product(left, high, low):
    top, rest = halves(left)
    both = jnp.concatenate([top, rest], axis=0)
    full = jnp.dot(both, high, preferred_element_type=jnp.float32)
    part = jnp.dot(top, low, preferred_element_type=jnp.float32)
    count = left.shape[0]
    return full[:count] + full[count:] + part


def payload_kernel(
    forces_hbm, particles_hbm, neighbours_hbm, out_hbm, forces_ref, particles_ref, neighbours_ref, sent, read, wrote
):
    col = lax.axis_index("col")
    start = pl.multiple_of((col // 2) * 8, 8)
    copies = [
        pltpu.make_async_copy(forces_hbm.at[:, pl.ds(start, 8), :], forces_ref, read.at[0]),
        pltpu.make_async_copy(particles_hbm, particles_ref, read.at[1]),
        pltpu.make_async_copy(neighbours_hbm, neighbours_ref, read.at[2]),
    ]
    for copy in copies:
        copy.start()
    lane = lax.broadcasted_iota(jnp.int32, (8, 128), 1)
    line = lax.broadcasted_iota(jnp.int32, (8, 128), 0)
    odd = jnp.full((8, 128), col % 2, jnp.int32) == 1
    for copy in copies:
        copy.wait()
    for half in range(2):
        sides = []
        for comp in range(COMPS):
            eight = forces_ref[comp, :, pl.ds(128 * half, 128)]
            sides.append(jnp.where(odd, pltpu.roll(eight, 4, axis=0), eight))
        place = jnp.concatenate(
            [particles_ref[:, pl.ds(128 * half, 128)], jnp.zeros((5, 128), jnp.float32)], axis=0
        )
        listed = jnp.full((8, 128), -1.0, jnp.float32)
        for entry in range(4):
            name = jnp.full((8, 128), neighbours_ref[half, entry], jnp.int32).astype(jnp.float32)
            listed = jnp.where(lane == 96 + entry, name, listed)
        for quarter in range(4):
            value = None
            for at, piece in enumerate([*sides, place]):
                turn = (SLICE * (at - quarter)) % 128
                piece = pltpu.roll(piece, turn, axis=1) if turn else piece
                value = piece if value is None else jnp.where(lane >= SLICE * at, piece, value)
            value = jnp.where((lane >= 96) & (line == 3), listed, value)
            sent[4 * half + quarter] = value[0:4]
    copies = [pltpu.make_async_copy(sent, out_hbm.at[row], wrote.at[row]) for row in range(ROWS)]
    for copy in copies:
        copy.start()
    for copy in copies:
        copy.wait()


def payload(forces, particles, neighbours):
    return pl.pallas_call(
        payload_kernel,
        out_shape=pltpu.HBM((ROWS, COLS, SHARE, 128), jnp.float32),
        in_specs=[IN_PLACE] * 3,
        out_specs=IN_PLACE,
        scratch_shapes=[
            pltpu.VMEM((COMPS, 8, 256), jnp.float32),
            pltpu.VMEM((COMPS, 256), jnp.float32),
            pltpu.SMEM((2, 4), jnp.int32),
            pltpu.VMEM((COLS, SHARE, 128), jnp.float32),
            pltpu.SemaphoreType.DMA((3,)),
            pltpu.SemaphoreType.DMA((ROWS,)),
        ],
        name="payload",
        compiler_params=GRANT,
    )(stay(forces), stay(particles), stay(neighbours))


def prepare_kernel(
    factor_ref, inverses_ref, carried_ref, fh_ref, fl_ref, lend_ref, ih_ref, il_ref, mine_ref, others_ref
):
    for panel in range(2):
        for comp in range(COMPS):
            for block in range(BLOCKS_DEV):
                rows = pl.ds(BLOCKS_DEV * comp + block, COLUMNS, stride=COMPS * BLOCKS_DEV)
                value = factor_ref[panel, rows, :]
                high, low = halves(value)
                pair = 2 * comp + block // 2
                lanes = pl.ds(128 * (block % 2), 128)
                fh_ref[panel, pair, :, lanes] = high
                fl_ref[panel, pair, :, lanes] = low
                if panel == 0 and comp == 1 and block == 0:
                    for quarter in range(4):
                        lend_ref[quarter] = value[128 * quarter : 128 * quarter + 128]
    for quarter in range(4):
        lend_ref[4 + quarter] = inverses_ref[1, :, pl.ds(128 * quarter, 128)]
    high, low = halves(inverses_ref[0])
    ih_ref[...] = high
    il_ref[...] = low
    owner = lax.broadcasted_iota(jnp.int32, (RHS, 128), 0) // SHARE
    own = owner == jnp.full((RHS, 128), lax.axis_index("col"), jnp.int32)
    for block in range(BLOCKS_DEV):
        for comp in range(COMPS):
            value = jnp.where(own, carried_ref[block, comp], 0.0)
            if block == 0:
                mine_ref[comp] = value
            else:
                others_ref[block - 1, comp] = value


def prepare(factor_rows, inverses, carried):
    panels = (2, 2 * COMPS, COLUMNS, 256)
    return pl.pallas_call(
        prepare_kernel,
        out_shape=(
            pltpu.HBM(panels, jnp.bfloat16),
            pltpu.HBM(panels, jnp.bfloat16),
            kept((8, 128, 128)),
            kept((128, COLUMNS), jnp.bfloat16),
            kept((128, COLUMNS), jnp.bfloat16),
            kept((COMPS, RHS, 128)),
            pltpu.HBM((BLOCKS_DEV - 1, COMPS, RHS, 128), jnp.float32),
        ),
        in_specs=[ON_CHIP] * 3,
        out_specs=(ON_CHIP,) * 7,
        name="prepare",
        compiler_params=GRANT,
    )(factor_rows, inverses, carried)


def fill(places_ref, source):
    for comp in range(COMPS):
        for group in range(ROWS):
            column = places_ref[comp, :, group : group + 1]
            source[comp, pl.ds(SLICE * group, SLICE), :] = jnp.broadcast_to(column, (SLICE, 128))


def couple(blocks, points_ref, flags_ref, push_ref, source_ref, high, low):
    width = 128 * len(blocks)
    totals = [None] * COMPS
    for tile in range(4):
        slot = tile % 2
        for where, block in enumerate(blocks):
            lanes = pl.ds(128 * where, 128)
            points = [points_ref[c : c + 1, pl.ds(128 * block, 128)] for c in range(COMPS)]
            flags = flags_ref[block : block + 1, :]
            for at in range(8):
                group = 8 * tile + at
                rows = pl.ds(SLICE * at, SLICE)
                spots = pl.ds(SLICE * group, SLICE)
                diff = [points[c] - source_ref[c, spots, :] for c in range(COMPS)]
                flag = jnp.broadcast_to(flags[:, 8 * group : 8 * group + 1], (SLICE, 128))
                radius = diff[0] * diff[0] + diff[1] * diff[1] + diff[2] * diff[2] + 1.0
                root = lax.rsqrt(radius)
                cube = root * root * root * flag
                iso = (radius + 1.0) * cube
                scaled = [diff[0] * cube, diff[1] * cube, diff[2] * cube]
                for n, (a, b) in enumerate(PAIRS):
                    value = scaled[a] * diff[b]
                    top, rest = halves(value + iso if a == b else value)
                    high[slot, n, rows, lanes] = top
                    low[slot, n, rows, lanes] = rest
        for n, (a, b) in enumerate(PAIRS):
            if a == b:
                left, first = push_ref[b, tile], push_ref[b, tile, 0:32]
            else:
                left = jnp.concatenate([push_ref[b, tile], push_ref[a, tile]], axis=0)
                first = jnp.concatenate(
                    [push_ref[b, tile, 0:32], push_ref[a, tile, 0:32]], axis=0
                )
            full = jnp.dot(left, high[slot, n, :, 0:width], preferred_element_type=jnp.float32)
            rest = jnp.dot(first, low[slot, n, :, 0:width], preferred_element_type=jnp.float32)
            add = full[0:32] + full[32:64] + rest[0:32]
            totals[a] = add if totals[a] is None else totals[a] + add
            if a != b:
                add = full[64:96] + full[96:128] + rest[32:64]
                totals[b] = add if totals[b] is None else totals[b] + add
    return totals


def near_first_kernel(
    got_ref, points_ref, mine_ref, out_ref, spread_ref, push_ref, places_ref, flags_ref, source_ref, high, low
):
    lane = lax.broadcasted_iota(jnp.int32, (RHS, 128), 1) // SLICE
    for quad in range(8):
        for comp in range(COMPS):
            joined = None
            for at in range(4):
                piece = got_ref[pl.ds(RHS * (4 * quad + at), RHS), :]
                turn = (SLICE * (at - comp)) % 128
                piece = pltpu.roll(piece, turn, axis=1) if turn else piece
                joined = piece if joined is None else jnp.where(lane == at, piece, joined)
            top, rest = halves(joined)
            lanes = pl.ds(128 * (quad % 2), 128)
            push_ref[comp, quad // 2, 0:32, lanes] = top
            push_ref[comp, quad // 2, 32:64, lanes] = rest
    for comp in range(COMPS):
        places_ref[comp] = got_ref[pl.ds(comp, ROWS, stride=RHS), :].T[96:128, :]
    fill(places_ref, source_ref)
    lists = got_ref[pl.ds(3, ROWS * COLS, stride=4), :].T[96:104, :]
    first = BLOCKS_DEV * lax.axis_index("row")
    for block in range(BLOCKS_DEV):
        name = jnp.full(lists.shape, first + block, jnp.int32).astype(jnp.float32)
        found = jnp.where(lists == name, 1.0, 0.0)
        for step in (1, 2, 4):
            found = jnp.maximum(found, pltpu.roll(found, ROWS * COLS - step, axis=1))
        flags_ref[block : block + 1, :] = jnp.max(found, axis=0, keepdims=True)
    totals = couple((0,), points_ref, flags_ref, push_ref, source_ref, high, low)
    for comp in range(COMPS):
        value = totals[comp] + mine_ref[comp]
        out_ref[comp] = value
        if comp == 0:
            for part in range(COLS):
                spread_ref[part] = value


def near_first(got, points, mine):
    return pl.pallas_call(
        near_first_kernel,
        out_shape=(
            kept((COMPS, RHS, 128)),
            kept((COLS, RHS, 128)),
            kept((COMPS, 4, 64, 256), jnp.bfloat16),
            kept((COMPS, SLICE, ROWS)),
            kept((BLOCKS_DEV, 256)),
        ),
        in_specs=[ON_CHIP] * 3,
        out_specs=(ON_CHIP,) * 5,
        scratch_shapes=[pltpu.VMEM((COMPS, ROWS * SLICE, 128), jnp.float32)]
        + [pltpu.VMEM((2, 6, 256, 128), jnp.bfloat16)] * 2,
        name="near_first",
        compiler_params=GRANT,
    )(keep(got), points, keep(mine))


def near_rest_kernel(
    points_ref, push_ref, places_ref, flags_ref, out_ref, source_ref, high, low
):
    fill(places_ref, source_ref)
    for blocks in ((1, 2, 3),):
        totals = couple(blocks, points_ref, flags_ref, push_ref, source_ref, high, low)
        for where, block in enumerate(blocks):
            for comp in range(COMPS):
                out_ref[block - 1, comp] = totals[comp][:, 128 * where : 128 * where + 128]


def near_rest(points, push, places, flags):
    return pl.pallas_call(
        near_rest_kernel,
        out_shape=kept((BLOCKS_DEV - 1, COMPS, RHS, 128)),
        in_specs=[ON_CHIP] * 4,
        out_specs=ON_CHIP,
        scratch_shapes=[pltpu.VMEM((COMPS, ROWS * SLICE, 128), jnp.float32)]
        + [pltpu.VMEM((2, 6, 256, 384), jnp.bfloat16)] * 2,
        name="near_rest",
        compiler_params=GRANT,
    )(points, keep(push), keep(places), keep(flags))


def total(parts_ref):
    value = parts_ref[0]
    for part in range(1, parts_ref.shape[0]):
        value = value + parts_ref[part]
    return value


def first_solve_kernel(parts_ref, ih_ref, il_ref, near_ref, out_ref):
    value = product(total(parts_ref), ih_ref[...], il_ref[...])
    for y in range(RING):
        sides = slice(EIGHT * y, EIGHT * y + EIGHT)
        for quarter in range(4):
            out_ref[y, pl.ds(EIGHT * quarter, EIGHT), :] = value[sides, 128 * quarter : 128 * quarter + 128]
        out_ref[y, pl.ds(32, EIGHT), :] = near_ref[1, pl.ds(EIGHT * y, EIGHT), :]


def first_solve(parts, ih, il, near):
    return pl.pallas_call(
        first_solve_kernel,
        out_shape=kept((RING, 40, 128)),
        in_specs=[ON_CHIP] * 4,
        out_specs=ON_CHIP,
        name="first_solve",
        compiler_params=GRANT,
    )(keep(parts), keep(ih), keep(il), keep(near))


def add_kernel(got_ref, out_ref):
    value = total(got_ref)[0:32]
    for part in range(DEPTH):
        out_ref[part] = value


def add(got):
    return pl.pallas_call(
        add_kernel,
        out_shape=kept((DEPTH, 32, 128)),
        in_specs=[ON_CHIP],
        out_specs=ON_CHIP,
        name="add",
        compiler_params=GRANT,
    )(keep(got))


def wide(value):
    return jnp.concatenate([value[EIGHT * q : EIGHT * q + EIGHT] for q in range(4)], axis=1)


def diagonal_kernel(parts_ref, got_ref, own_ref, one_ref, two_ref, three_ref, answer_ref, out_ref):
    value = total(parts_ref)
    answer_ref[...] = value
    answer = wide(value)
    y = lax.axis_index("row") % RING
    for step, tiles in enumerate((own_ref, one_ref, two_ref, three_ref)):
        columns = jnp.concatenate([tiles[quarter] for quarter in range(4)], axis=0)
        base = got_ref[(y + step) % RING, pl.ds(32, EIGHT), :]
        value = base - product(answer, *halves(columns))
        for part in range(COLS):
            out_ref[part, pl.ds(EIGHT * step, EIGHT), :] = value


def diagonal(parts, got, tiles):
    return pl.pallas_call(
        diagonal_kernel,
        out_shape=(kept((32, 128)), kept((COLS, 32, 128))),
        in_specs=[ON_CHIP] * 6,
        out_specs=(ON_CHIP,) * 2,
        name="diagonal",
        compiler_params=GRANT,
    )(keep(parts), keep(got), *[keep(tile) for tile in tiles])


def second_solve_kernel(parts_ref, own_ref, one_ref, two_ref, three_ref, out_ref):
    diag = total(parts_ref)
    value = None
    for step, tiles in enumerate((own_ref, one_ref, two_ref, three_ref)):
        inverse = jnp.concatenate([tiles[4 + quarter] for quarter in range(4)], axis=1)
        add = product(diag[EIGHT * step : EIGHT * step + EIGHT], *halves(inverse))
        value = add if value is None else value + add
    for part in range(DEPTH):
        for quarter in range(4):
            out_ref[part, pl.ds(EIGHT * quarter, EIGHT), :] = value[:, 128 * quarter : 128 * quarter + 128]


def second_solve(parts, tiles):
    return pl.pallas_call(
        second_solve_kernel,
        out_shape=kept((DEPTH, 32, 128)),
        in_specs=[ON_CHIP] * 5,
        out_specs=ON_CHIP,
        name="second_solve",
        compiler_params=GRANT,
    )(keep(parts), *[keep(tile) for tile in tiles])


def gather_kernel(parts_ref, first_ref, out_ref):
    second = total(parts_ref)
    for y in range(RING):
        out_ref[y, 0:32] = first_ref[...]
        out_ref[y, 32:64] = second


def gather(parts, first):
    return pl.pallas_call(
        gather_kernel,
        out_shape=kept((RING, 64, 128)),
        in_specs=[ON_CHIP] * 2,
        out_specs=ON_CHIP,
        name="gather",
        compiler_params=GRANT,
    )(keep(parts), keep(first))


def whole(got_ref, panel):
    columns = []
    for quarter in range(4):
        rows = pl.ds(32 * panel + EIGHT * quarter, EIGHT)
        columns.append(jnp.concatenate([got_ref[y, rows, :] for y in range(RING)], axis=0))
    return jnp.concatenate(columns, axis=1)


def change_kernel(
    got_ref, fh_hbm, fl_hbm, others_hbm, first_ref, rest_ref, out_ref, answers_hbm,
    high, low, others, both, read, extra
):
    jobs, copies = [], []
    for comp in range(COMPS):
        for pair in range(2):
            for panel in range(2):
                at = len(jobs)
                hidden = pair == 0 and comp <= panel
                lanes = pl.ds(128, 128) if hidden else pl.ds(0, 256)
                jobs.append((comp, pair, panel, hidden, lanes))
                for side, (source, target) in enumerate(((fh_hbm, high), (fl_hbm, low))):
                    copies.append(
                        pltpu.make_async_copy(
                            source.at[panel, 2 * comp + pair, :, lanes],
                            target.at[at, :, lanes],
                            read.at[2 * at + side],
                        )
                    )
    carry = pltpu.make_async_copy(others_hbm, others, extra.at[0])
    carry.start()
    ahead = 24
    for copy in copies[:ahead]:
        copy.start()
    sides = [whole(got_ref, panel) for panel in range(2)]
    both[0], both[1] = sides
    answer = pltpu.make_async_copy(both, answers_hbm, extra.at[1])
    answer.start()
    carry.wait()
    group = 6
    for first in range(0, len(jobs), group):
        for copy in copies[2 * first : 2 * (first + group)]:
            copy.wait()
        for copy in copies[2 * first + ahead : 2 * (first + group) + ahead]:
            copy.start()
        moved = {}
        for at in range(first, first + group):
            comp, pair, panel, hidden, lanes = jobs[at]
            moved[comp, pair, panel] = product(sides[panel], high[at, :, lanes], low[at, :, lanes])
        for comp, pair, panel in list(moved):
            if panel == 0:
                continue
            for where in range(2):
                block = 2 * pair + where
                if block == 0:
                    value = first_ref[comp]
                else:
                    value = rest_ref[block - 1, comp] + others[block - 1, comp]
                for index in range(2):
                    part = moved[comp, pair, index]
                    if block > 0 or comp > index:
                        start = part.shape[1] - 256 + 128 * where
                        value = value - part[:, start : start + 128]
                for part in range(COLS):
                    out_ref[part, block, comp] = value[SHARE * part : SHARE * part + SHARE]
    answer.wait()


def change(got, fh, fl, others, first, rest):
    return pl.pallas_call(
        change_kernel,
        out_shape=(
            kept((COLS, BLOCKS_DEV, COMPS, SHARE, 128)),
            pltpu.HBM((2, RHS, COLUMNS), jnp.float32),
        ),
        in_specs=[ON_CHIP, IN_PLACE, IN_PLACE, IN_PLACE, ON_CHIP, ON_CHIP],
        out_specs=(ON_CHIP, IN_PLACE),
        scratch_shapes=[
            pltpu.VMEM((4 * COMPS, COLUMNS, 256), jnp.bfloat16),
            pltpu.VMEM((4 * COMPS, COLUMNS, 256), jnp.bfloat16),
            pltpu.VMEM((BLOCKS_DEV - 1, COMPS, RHS, 128), jnp.float32),
            pltpu.VMEM((2, RHS, COLUMNS), jnp.float32),
            pltpu.SemaphoreType.DMA((8 * COMPS,)),
            pltpu.SemaphoreType.DMA((2,)),
        ],
        name="change",
        compiler_params=GRANT,
    )(keep(got), stay(fh), stay(fl), stay(others), keep(first), keep(rest))


def along(array, groups):
    return lax.all_to_all(array, "row", 0, 0, axis_index_groups=groups, tiled=True)


def body(obstacles, particles, forces, neighbours, carried, factor, inverses):
    ring = [[RING * z + y for y in range(RING)] for z in range(DEPTH)]
    line = [[RING * z + y for z in range(DEPTH)] for y in range(RING)]
    sent = payload(forces, particles, neighbours).reshape(ROWS * COLS, SHARE, 128)
    got = lax.all_to_all(sent, ("row", "col"), 0, 0, tiled=True).reshape(ROWS * RHS, 128)
    rows = factor.transpose(0, 1, 3, 2, 4).reshape(2, COLUMNS * COMPS * BLOCKS_DEV, 128)
    fh, fl, lend, ih, il, mine, others = prepare(rows, inverses, carried)
    tiles = [lend]
    for step in range(1, RING):
        pairs = [(RING * z + (y + step) % RING, RING * z + y) for z in range(DEPTH) for y in range(RING)]
        tiles.append(lax.ppermute(lend, "row", pairs))
    near0, spread, push, places, flags = near_first(got, obstacles, mine)
    parts = lax.all_to_all(spread, "col", 0, 0, tiled=True)
    rest = near_rest(obstacles, push, places, flags)
    shares = along(first_solve(parts, ih, il, near0), ring)
    shares, rest, *tiles = lax.optimization_barrier((shares, rest, *tiles))
    parts = along(add(shares), line)
    first, spread = diagonal(parts, shares, tiles)
    parts = lax.all_to_all(spread, "col", 0, 0, tiled=True)
    parts = along(second_solve(parts, tiles), line)
    shares = along(gather(parts, first), ring)
    part, answers = change(shares, fh, fl, others, near0, rest)
    back = lax.all_to_all(part, "col", 0, 0, tiled=True)
    return (answers, jnp.sum(back, axis=0))


def solution(mesh):
    in_specs = (
        P(None, "row"),
        P(None, "row"),
        P(None, None, "row"),
        P("row", "col"),
        P("row", None, None, None),
        P(None, "col", "row", None, None),
        P(None, "row", "col"),
    )
    out_specs = (P(None, None, "col"), P("row", None, "col", None))
    return jax.shard_map(body, mesh=mesh, in_specs=in_specs, out_specs=out_specs, check_vma=False)
```
